32 devices in a mesh: groups: 2 (over y), section: 4 (over z), mp: 4 (over x, core).
Axes of the slice: x: 2, y: 2, z: 4, core: 2. Of those that a mesh axis runs over, the one named last changes fastest.
Arguments:
- memory: bfloat16 [16, 8, 4096], P(('section', 'mp'), 'groups'), parts along dimension 1, may hold values from -6 to 6
- decoder_in: bfloat16 [8, 32, 4096], P('groups'), parts along dimension 0, may hold values from -6 to 6
- cotangent: bfloat16 [8, 32, 4096], P('groups'), parts along dimension 0, may hold values from -6 to 6
- src_lengths: int32 [8, 4], P('groups'), parts along dimension 0, may hold values from 1 to 8, 16 in all within a row
- tgt_segments: int32 [8, 32], P('groups'), parts along dimension 0, may hold values from 0 to 3, never falling along the last dimension, each value on 1 to 16 neighbouring positions
- seeds: int32 [8, 4], P('groups', 'section'), parts along dimension 0, may hold values from 0 to 1073741823
- w_query: bfloat16 [4, 4096, 2048], P('section', None, 'mp'), may hold values from -0.09375 to 0.09375
- w_key: bfloat16 [4, 4096, 2048], P('section', None, 'mp'), may hold values from -0.09375 to 0.09375
- w_value: bfloat16 [4, 4096, 2048], P('section', None, 'mp'), may hold values from -0.09375 to 0.09375
- w_out: bfloat16 [4, 2048, 4096], P('section', 'mp'), may hold values from -0.125 to 0.125
Outputs:
- section_out: bfloat16 [4, 8, 32, 4096], P('section', 'groups', None, 'mp'), parts along dimension 1
- mem_grad: float32 [16, 8, 4096], P(('section', 'mp'), 'groups'), parts along dimension 1
The draws below stay inside these ranges and needn't reach their ends.
There are 2 independent parts, one for each index of `groups`. The reference program is written for one: setup_inputs(seed, part) draws one part's arguments, and reference() takes and returns one part's arrays. A program takes and returns all parts, laid end to end along the dimension named above; an argument that names none is the same for every part. Nothing has to cross between parts.
Inputs may be any that keep to these rules, and one draw needn't show every extreme that they name: `src_lengths`: in each micro-batch the 4 lengths sum to 16, and the longest is exactly 8. `tgt_segments`: ids never fall along a micro-batch's tokens.
All inputs are finite; a program needn't handle non-finite values.
Results may differ from the reference program's by a relative error of at most 0.02.
Values may be sent and summed in bfloat16 or wider, within the bound.
No kernel may reach another device: no remote copies, remote signals or barrier semaphores. Data moves between devices by JAX's collectives and lax.ppermute only.
A program may use at most 128 MiB of HBM per device.

```python
import math
import jax
import jax.numpy as jnp
import numpy as np
from jax import lax

D = 4096
HEADS = 8
HD = 256
MB = 4
TGT = 32
DOCS = 4
SRC = 16
SECTIONS = 4
N_MP = 4


def draw_memory(key, part):
    base_vals = jnp.clip(jax.random.normal(jax.random.fold_in(key, 101), (SRC, MB, D), jnp.float32), -6.0, 6.0)
    return base_vals.astype(jnp.bfloat16)


def draw_decoder_in(key, part):
    base_vals = jnp.clip(jax.random.normal(jax.random.fold_in(key, 211), (MB, TGT, D), jnp.float32), -6.0, 6.0)
    return base_vals.astype(jnp.bfloat16)


def plant(entries, rng, low, top_value):
    longest = entries.shape.index(max(entries.shape))
    spots = []
    for shift in (0, 1):
        where = [jax.random.randint(jax.random.fold_in(rng, axis), (), 0, length) for axis, length in enumerate(entries.shape)]
        where[longest] = (where[longest] + shift) % entries.shape[longest]
        spots.append(tuple(where))
    return entries.at[spots[0]].set(low).at[spots[1]].set(top_value)


def block_scale(stream_key, extent, shards, least, high):
    def one(dim, shards_of):
        heights = jax.random.uniform(jax.random.fold_in(jax.random.fold_in(stream_key, 6), dim), (shards_of,), jnp.float32, least / len(shards), high / len(shards))
        return jnp.repeat(jnp.exp(heights), extent[dim] // shards_of).reshape((-1,) + (1,) * (len(extent) - dim - 1))

    loudness = one(*shards[0])
    for cut in shards[1:]:
        loudness = loudness * one(*cut)
    return loudness


def profile(count, total, bound, skew):
    portions = [(1 << 20) // math.isqrt(standing ** skew) + 1 for standing in range(2, count + 1)]
    rest, holding = total - bound - (count - 1), [1] * (count - 1)
    while rest > 0:
        free = [i for i in range(count - 1) if holding[i] < bound]
        mass, remaining = sum([portions[i] for i in free]), rest
        for i in free:
            addition = min(bound - holding[i], max(1, remaining * portions[i] // mass), rest)
            holding[i] = holding[i] + addition
            rest = rest - addition
    return np.array([bound] + holding)


def ragged(own_key, count, total, most, skew):
    if count == 2:
        one = jax.random.randint(own_key, (), max(1, total - most), min(most, total - 1) + 1)
        return jnp.stack([one, total - one])
    sizes = jnp.asarray(profile(count, total, most, skew), jnp.int32)
    pairs = (count - 1) // 2
    donor, sink = sizes[1:1 + 2 * pairs:2], sizes[2:2 + 2 * pairs:2]
    room = jnp.minimum(donor - 1, most - sink)
    shifted = jax.random.randint(jax.random.fold_in(own_key, 1), (pairs,), 0, 1 << 20) % (room + 1)
    sizes = sizes.at[1:1 + 2 * pairs:2].set(donor - shifted).at[2:2 + 2 * pairs:2].set(sink + shifted)
    return sizes[jax.random.permutation(jax.random.fold_in(own_key, 2), count)]


def scatter_about(key, extent, spread, most, pieces=(), kind=jnp.bfloat16):
    entries = spread * jax.random.normal(key, extent, jnp.float32)
    if pieces:
        entries = entries * block_scale(key, extent, pieces, -0.22, 0.18)
    return jnp.clip(entries, -most, most).astype(kind)


def setup_inputs(seed: int = 0, part: int = 0) -> dict:
    arg_keys = jax.random.split(jax.random.key(seed), 11)
    part_keys = jax.random.split(jax.random.fold_in(arg_keys[10], part), 11)
    return {
        "memory": draw_memory(jax.random.fold_in(jax.random.fold_in(arg_keys[10], part), 71), part),
        "decoder_in": draw_decoder_in(jax.random.fold_in(jax.random.fold_in(arg_keys[10], part), 71), part),
        "cotangent": scatter_about(part_keys[2], (MB, TGT, D), 1.0, 6.0),
        "src_lengths": jax.vmap(lambda own: ragged(own, DOCS, SRC, SRC // 2, 2))(jax.random.split(part_keys[3], MB)).reshape((MB, DOCS)).astype(jnp.int32),
        "tgt_segments": jax.vmap(lambda own: jnp.searchsorted(jnp.cumsum(ragged(own, DOCS, TGT, TGT // 2, 2)), jnp.arange(TGT), side="right"))(jax.random.split(part_keys[4], MB)).reshape((MB, TGT)).astype(jnp.int32),
        "seeds": plant(jax.random.randint(part_keys[5], (MB, SECTIONS), 0, 1073741824), jax.random.fold_in(part_keys[5], 1), 0, 1073741823).astype(jnp.int32),
        "w_query": scatter_about(arg_keys[6], (SECTIONS, D, HEADS * HD), D ** -0.5, 0.09375, ((0, 4), (2, 4))),
        "w_key": scatter_about(arg_keys[7], (SECTIONS, D, HEADS * HD), D ** -0.5, 0.09375, ((0, 4), (2, 4))),
        "w_value": scatter_about(arg_keys[8], (SECTIONS, D, HEADS * HD), D ** -0.5, 0.09375, ((0, 4), (2, 4))),
        "w_out": scatter_about(arg_keys[9], (SECTIONS, HEADS * HD, D), (HEADS * HD) ** -0.5, 0.125, ((0, 4), (1, 4))),
    }


NEG_FILL = -1e+30
KEEP_SCALE = 8.0 / 7.0

def shifted_right(source_bits, amount):
    return lax.shift_right_logical(source_bits, jnp.full(source_bits.shape, amount, jnp.int32))

def keep_factor(seed_value, row_count, col_count):
    position = jnp.arange(row_count, dtype=jnp.int32)[:, None] * col_count + jnp.arange(col_count, dtype=jnp.int32)[None, :]
    hashed = position ^ seed_value * 1640531527
    hashed = hashed ^ shifted_right(hashed, 16)
    hashed = hashed * 2146121005
    hashed = hashed ^ shifted_right(hashed, 15)
    hashed = hashed * 1911520717
    hashed = hashed ^ shifted_right(hashed, 16)
    is_kept = shifted_right(hashed, 8) & 7 != 0
    return jnp.where(is_kept, KEEP_SCALE, 0.0).astype(jnp.float32)

def document_rows(lengths_row, src_rows):
    doc_ends = jnp.cumsum(lengths_row).astype(jnp.int32)
    row_index = jnp.arange(src_rows, dtype=jnp.int32)
    return lax.optimization_barrier(jnp.sum((doc_ends[None, :] <= row_index[:, None]).astype(jnp.int32), axis=1)).astype(jnp.int32)

def rounded_copy(source_vals):
    return lax.optimization_barrier(source_vals.astype(jnp.bfloat16))

def softmax_rows(query_heads, key_heads, allowed):
    scores = jnp.einsum('thd,shd->hts', query_heads.astype(jnp.float32), key_heads.astype(jnp.float32)) * (1.0 / math.sqrt(HD))
    scores = jnp.where(allowed[None, :, :], scores, NEG_FILL)
    row_peak = lax.optimization_barrier(jnp.max(scores, axis=2, keepdims=True))
    exp_terms = jnp.exp(scores - row_peak)
    return exp_terms / lax.optimization_barrier(jnp.sum(exp_terms, axis=2, keepdims=True))

def grouped_sum(left_groups, right_groups):
    group_terms = jnp.einsum('tgk,gkd->gtd', left_groups.astype(jnp.float32), right_groups.astype(jnp.float32))
    return lax.optimization_barrier(jnp.sum(rounded_copy(group_terms).astype(jnp.float32), axis=0))

def layer_parts(current, source_rows, layer_index, allowed, w_query, w_key, w_value):
    key_rows = jnp.dot(source_rows, w_key[layer_index], preferred_element_type=jnp.float32).astype(jnp.bfloat16)
    value_rows = jnp.dot(source_rows, w_value[layer_index], preferred_element_type=jnp.float32).astype(jnp.bfloat16)
    query_rows = jnp.dot(current, w_query[layer_index], preferred_element_type=jnp.float32).astype(jnp.bfloat16)
    key_heads = key_rows.reshape(SRC, HEADS, HD)
    value_heads = value_rows.reshape(SRC, HEADS, HD)
    query_heads = query_rows.reshape(TGT, HEADS, HD)
    prob_rows = softmax_rows(query_heads, key_heads, allowed)
    return (key_heads, value_heads, query_heads, prob_rows)

def reference(memory, decoder_in, cotangent, src_lengths, tgt_segments, seeds, w_query, w_key, w_value, w_out):
    heads_dim = HEADS * HD
    group_dim = heads_dim // N_MP
    score_scale = 1.0 / math.sqrt(HD)
    mem_grad = jnp.zeros((SRC, MB, D), jnp.float32)
    kept_out = [[None] * MB for layer_index in range(SECTIONS)]
    for micro_index in range(MB):
        doc_ids = document_rows(src_lengths[micro_index], SRC)
        allowed = tgt_segments[micro_index][:, None] == doc_ids[None, :]
        source_rows = memory[:, micro_index, :]
        current = decoder_in[micro_index]
        saved_inputs = []
        for layer_index in range(SECTIONS):
            key_heads, value_heads, query_heads, prob_rows = layer_parts(current, source_rows, layer_index, allowed, w_query, w_key, w_value)
            weights_b = rounded_copy(prob_rows).astype(jnp.float32)
            attended = jnp.einsum('hts,shd->thd', weights_b, value_heads.astype(jnp.float32)).astype(jnp.bfloat16)
            summed = grouped_sum(attended.reshape(TGT, N_MP, group_dim), w_out[layer_index].reshape(N_MP, group_dim, D))
            factor = keep_factor(seeds[micro_index, layer_index], TGT, D)
            following = (current.astype(jnp.float32) + factor * summed).astype(jnp.bfloat16)
            saved_inputs.append(current)
            kept_out[layer_index][micro_index] = following
            current = following
        grad_now = cotangent[micro_index]
        for layer_index in reversed(range(SECTIONS)):
            current = saved_inputs[layer_index]
            key_heads, value_heads, query_heads, prob_rows = layer_parts(current, source_rows, layer_index, allowed, w_query, w_key, w_value)
            weights_b = rounded_copy(prob_rows).astype(jnp.float32)
            factor = keep_factor(seeds[micro_index, layer_index], TGT, D)
            d_out = (grad_now.astype(jnp.float32) * factor).astype(jnp.bfloat16)
            d_att = jnp.dot(d_out, w_out[layer_index].T, preferred_element_type=jnp.float32).astype(jnp.bfloat16)
            d_heads = d_att.reshape(TGT, HEADS, HD).astype(jnp.float32)
            d_probs = jnp.einsum('thd,shd->hts', d_heads, value_heads.astype(jnp.float32))
            inner_sum = lax.optimization_barrier(jnp.sum(prob_rows * d_probs, axis=2, keepdims=True))
            d_scores = rounded_copy(prob_rows * (d_probs - inner_sum) * score_scale).astype(jnp.float32)
            d_query = jnp.einsum('hts,shd->thd', d_scores, key_heads.astype(jnp.float32)).astype(jnp.bfloat16)
            d_keys = jnp.einsum('hts,thd->shd', d_scores, query_heads.astype(jnp.float32)).astype(jnp.bfloat16).reshape(SRC, heads_dim)
            d_values = jnp.einsum('hts,thd->shd', weights_b, d_heads).astype(jnp.bfloat16).reshape(SRC, heads_dim)
            query_groups = jnp.transpose(w_query[layer_index].reshape(D, N_MP, group_dim), (1, 2, 0))
            back_sum = grouped_sum(d_query.reshape(TGT, N_MP, group_dim), query_groups)
            grad_now = (grad_now.astype(jnp.float32) + back_sum).astype(jnp.bfloat16)
            term_rows = jnp.dot(d_keys, w_key[layer_index].T, preferred_element_type=jnp.float32) + jnp.dot(d_values, w_value[layer_index].T, preferred_element_type=jnp.float32)
            mem_grad = mem_grad.at[:, micro_index, :].add(term_rows)
    section_out = jnp.stack([jnp.stack(kept_out[layer_index], axis=0) for layer_index in range(SECTIONS)], axis=0)
    return (section_out, mem_grad)
```

```python
import math

import jax
import jax.numpy as jnp
from jax import lax
from jax.sharding import PartitionSpec as P

HD = 256
NEG_FILL = -1e30
KEEP_SCALE = 8.0 / 7.0
BF = jnp.bfloat16
F32 = jnp.float32


def shifted_right(source_bits, amount):
    return lax.shift_right_logical(source_bits, jnp.full(source_bits.shape, amount, jnp.int32))


def keep_factor(seed_value, first_row, row_count, col_count):
    position = (
        (first_row + jnp.arange(row_count, dtype=jnp.int32))[:, None] * col_count
        + jnp.arange(col_count, dtype=jnp.int32)[None, :]
    )
    hashed = position ^ seed_value * 1640531527
    hashed = hashed ^ shifted_right(hashed, 16)
    hashed = hashed * 2146121005
    hashed = hashed ^ shifted_right(hashed, 15)
    hashed = hashed * 1911520717
    hashed = hashed ^ shifted_right(hashed, 16)
    is_kept = shifted_right(hashed, 8) & 7 != 0
    return jnp.where(is_kept, KEEP_SCALE, 0.0).astype(F32)


def swap(array, axis, k):
    size = lax.axis_size(axis)
    return lax.ppermute(array, axis, [(i, i ^ k) for i in range(size)])


def gather_swaps(array, axis, ks):
    return [array if k == 0 else swap(array, axis, k) for k in ks]


def dot_f32(spec, left, right):
    return jnp.einsum(spec, left, right, preferred_element_type=F32)


def softmax_rows(scores, allowed):
    scores = jnp.where(allowed, scores, NEG_FILL)
    exp_terms = jnp.exp(scores - jnp.max(scores, axis=-1, keepdims=True))
    return exp_terms / jnp.sum(exp_terms, axis=-1, keepdims=True)


def per_device(
    memory, decoder_in, cotangent, src_lengths, tgt_segments, seeds, w_query, w_key, w_value, w_out
):
    micro_count, tgt_rows, dim = decoder_in.shape
    local_cols = w_query.shape[2]
    heads = local_cols // HD
    scale = 1.0 / math.sqrt(HD)
    sections = lax.axis_size("section")
    n_mp = lax.axis_size("mp")
    section = lax.axis_index("section")
    me = lax.axis_index("mp")
    share = n_mp // micro_count
    rows = tgt_rows // share
    src = sections * n_mp
    wq, wk, wv, wo = w_query[0], w_key[0], w_value[0], w_out[0]

    over_z = jnp.concatenate(gather_swaps(memory, "section", range(sections)), axis=0)
    over_x = jnp.stack(gather_swaps(over_z, "mp", range(0, n_mp, 2)), axis=1)
    over_core = jnp.stack(gather_swaps(over_x, "mp", range(2)), axis=2)
    mem_rows = over_core.reshape(src, micro_count, dim)

    def row_ids(device):
        a = jnp.arange(sections, dtype=jnp.int32)[:, None]
        j = jnp.arange(n_mp, dtype=jnp.int32)[None, :]
        return ((section ^ a) * n_mp + (device ^ j)).reshape(src)

    doc_ends = jnp.cumsum(src_lengths, axis=1)

    def allowed_of(owner, heads_owner):
        micro = owner // share
        ends = lax.dynamic_index_in_dim(doc_ends, micro, 0, keepdims=False)
        segments = lax.dynamic_index_in_dim(tgt_segments, micro, 0, keepdims=False)
        segments = lax.dynamic_slice_in_dim(segments, (owner % share) * rows, rows, 0)
        ids = row_ids(heads_owner)
        docs = jnp.sum((ends[None, :] <= ids[:, None]).astype(jnp.int32), axis=1)
        return segments[:, None] == docs[None, :]

    keys = dot_f32("rbd,dk->brk", mem_rows, wk).astype(BF)
    values = dot_f32("rbd,dk->brk", mem_rows, wv).astype(BF)

    def by_owner(array):
        return jnp.stack(
            [
                lax.dynamic_index_in_dim(array, (me ^ j) // share, 0, keepdims=False)
                for j in range(n_mp)
            ]
        )

    keys = by_owner(keys).reshape(n_mp, src, heads, HD)
    values = by_owner(values).reshape(n_mp, src, heads, HD)
    out_fold = jnp.stack(
        [
            dot_f32("jsk,kd->jsd", values[:, :, h], wo[h * HD : (h + 1) * HD]).astype(BF)
            for h in range(heads)
        ],
        axis=1,
    )
    query_fold = jnp.stack(
        [
            dot_f32("jsk,dk->jsd", keys[:, :, h], wq[:, h * HD : (h + 1) * HD]).astype(BF)
            for h in range(heads)
        ],
        axis=1,
    )

    def to_owners(fold):
        blocks = [fold[j] if j == 0 else swap(fold[j], "mp", j) for j in range(n_mp)]
        return jnp.stack(blocks).reshape(n_mp * heads * src, dim)

    out_fold = to_owners(out_fold)
    query_fold = to_owners(query_fold)
    allowed = jnp.stack([allowed_of(me, me ^ k) for k in range(n_mp)], axis=1)
    allowed = jnp.broadcast_to(allowed[:, :, None, :], (rows, n_mp, heads, src))

    my_micro = me // share
    my_first = (me % share) * rows

    def mine(array):
        part = lax.dynamic_index_in_dim(array, my_micro, 0, keepdims=False)
        return lax.dynamic_slice_in_dim(part, my_first, rows, 0)

    factor = keep_factor(seeds[my_micro, 0], my_first, rows, dim)

    def probs(current):
        scores = dot_f32("td,kd->tk", current, query_fold) * scale
        return softmax_rows(scores.reshape(rows, n_mp, heads, src), allowed)

    def layer(current):
        weights = probs(current).astype(BF).reshape(rows, n_mp * heads * src)
        summed = dot_f32("tk,kd->td", weights, out_fold)
        return (current.astype(F32) + factor * summed).astype(BF)

    current = mine(decoder_in)
    for step in range(sections - 1):
        came = lax.ppermute(layer(current), "section", [(step, step + 1)])
        current = jnp.where(section == step + 1, came, current)
    following = layer(current)
    prob_rows = probs(current)

    grad = mine(cotangent)

    def dropped(grad):
        return (grad.astype(F32) * factor).astype(BF)

    for step in range(sections - 1, 0, -1):
        d_probs = dot_f32("td,kd->tk", dropped(grad), out_fold).reshape(prob_rows.shape)
        inner = jnp.sum(prob_rows * d_probs, axis=-1, keepdims=True)
        d_scores = (prob_rows * (d_probs - inner) * scale).astype(BF)
        back = dot_f32("tk,kd->td", d_scores.reshape(rows, -1), query_fold)
        before = (grad.astype(F32) + back).astype(BF)
        came = lax.ppermute(before, "section", [(step, step - 1)])
        grad = jnp.where(section == step - 1, came, grad)

    def all_tokens(array):
        over_x = jnp.stack(gather_swaps(array, "mp", range(0, n_mp, 2)))
        return jnp.stack(gather_swaps(over_x, "mp", range(2)), axis=1).reshape(n_mp * rows, dim)

    every_x = all_tokens(current)
    every_d_out = all_tokens(dropped(grad))
    query = jnp.dot(every_x, wq, preferred_element_type=F32).astype(BF)
    query = query.reshape(n_mp, rows, heads, HD)
    d_att = dot_f32("td,kd->tk", every_d_out, wo).astype(BF).reshape(n_mp, rows, heads, HD)
    own_allowed = jnp.stack([allowed_of(me ^ j, me) for j in range(n_mp)])[:, None]
    own_probs = softmax_rows(dot_f32("jthk,jshk->jhts", query, keys) * scale, own_allowed)
    d_probs = dot_f32("jthk,jshk->jhts", d_att, values)
    inner = jnp.sum(own_probs * d_probs, axis=-1, keepdims=True)
    d_scores = (own_probs * (d_probs - inner) * scale).astype(BF)
    d_keys = dot_f32("jhts,jthk->jshk", d_scores, query).reshape(n_mp, src, local_cols)
    d_values = dot_f32("jhts,jthk->jshk", own_probs.astype(BF), d_att)
    d_values = d_values.reshape(n_mp, src, local_cols)

    def by_micro(array):
        parts = []
        for micro in range(micro_count):
            total = 0.0
            for q in range(share):
                owner = me ^ (micro * share + q)
                total = total + lax.dynamic_index_in_dim(array, owner, 0, keepdims=False)
            parts.append(total.astype(BF))
        return jnp.stack(parts, axis=1)

    terms = dot_f32("rbk,dk->rbd", by_micro(d_keys), wk) + dot_f32(
        "rbk,dk->rbd", by_micro(d_values), wv
    )
    terms = terms.reshape(sections, n_mp // 2, 2, micro_count, dim)
    half = terms[:, :, 0] + swap(terms[:, :, 1].astype(BF), "mp", 1).astype(F32)
    total = half[:, 0]
    for j in range(1, n_mp // 2):
        total = total + swap(half[:, j].astype(BF), "mp", 2 * j).astype(F32)
    mem_grad = total[0]
    for a in range(1, sections):
        mem_grad = mem_grad + swap(total[a].astype(BF), "section", a).astype(F32)

    out_cols = dim // n_mp
    following = following.reshape(rows, n_mp, out_cols)
    blocks = []
    for j in range(n_mp):
        part = lax.dynamic_index_in_dim(following, me ^ j, 1, keepdims=False)
        blocks.append(part if j == 0 else swap(part, "mp", j))
    stacked = jnp.stack(blocks)
    ordered = [
        lax.dynamic_index_in_dim(stacked, me ^ owner, 0, keepdims=False) for owner in range(n_mp)
    ]
    section_out = jnp.stack(ordered).reshape(1, micro_count, tgt_rows, out_cols)
    return (section_out, mem_grad[None])


def solution(mesh):
    return jax.shard_map(
        per_device,
        mesh=mesh,
        in_specs=(
            P(("section", "mp"), "groups", None),
            P("groups", None, None),
            P("groups", None, None),
            P("groups", None),
            P("groups", None),
            P("groups", "section"),
            P("section", None, "mp"),
            P("section", None, "mp"),
            P("section", None, "mp"),
            P("section", "mp", None),
        ),
        out_specs=(P("section", "groups", None, "mp"), P(("section", "mp"), "groups", None)),
        check_vma=False,
    )
```

```python
import functools
import math

import jax
import jax.numpy as jnp
from jax import lax
from jax.experimental import pallas as pl
from jax.experimental.pallas import tpu as pltpu
from jax.sharding import PartitionSpec as P

HD = 256
NEG_FILL = -1e30
KEEP_SCALE = 8.0 / 7.0
BF = jnp.bfloat16
F32 = jnp.float32


def shifted_right(source_bits, amount):
    return lax.shift_right_logical(source_bits, jnp.full(source_bits.shape, amount, jnp.int32))


def keep_factor(seed_value, first_row, row_count, col_count):
    position = (
        (first_row + jnp.arange(row_count, dtype=jnp.int32))[:, None] * col_count
        + jnp.arange(col_count, dtype=jnp.int32)[None, :]
    )
    hashed = position ^ seed_value * 1640531527
    hashed = hashed ^ shifted_right(hashed, 16)
    hashed = hashed * 2146121005
    hashed = hashed ^ shifted_right(hashed, 15)
    hashed = hashed * 1911520717
    hashed = hashed ^ shifted_right(hashed, 16)
    is_kept = shifted_right(hashed, 8) & 7 != 0
    return jnp.where(is_kept, KEEP_SCALE, 0.0).astype(F32)


def swap(array, axis, k):
    size = lax.axis_size(axis)
    return lax.ppermute(array, axis, [(i, i ^ k) for i in range(size)])


def gather_swaps(array, axis, ks):
    return [array if k == 0 else swap(array, axis, k) for k in ks]


def dot_f32(spec, left, right):
    return jnp.einsum(spec, left, right, preferred_element_type=F32)


def softmax_rows(scores, allowed):
    scores = jnp.where(allowed, scores, NEG_FILL)
    exp_terms = jnp.exp(scores - jnp.max(scores, axis=-1, keepdims=True))
    return exp_terms / jnp.sum(exp_terms, axis=-1, keepdims=True)

TRANSPOSED = (((1,), (1,)), ((), ()))
FIRST = (((0,), (0,)), ((), ()))
MEBI = 1024 * 1024


def product(left, right, dims):
    return lax.dot_general(left, right, dims, preferred_element_type=F32)


def scores_of(folds, tokens):
    return jnp.concatenate([product(fold[...], tokens, TRANSPOSED) for fold in folds], axis=0)


def spread(weights, folds):
    size = weights.shape[0] // len(folds)
    turned = jnp.transpose(weights)
    total = None
    for k, fold in enumerate(folds):
        part = product(turned[:, k * size : (k + 1) * size].astype(BF), fold[...], PLAIN)
        total = part if total is None else total + part
    return total


PLAIN = (((1,), (0,)), ((), ()))


def probs_of(query_folds, tokens, allowed, scale, src):
    scores = scores_of(query_folds, tokens) * scale
    scores = jnp.where(allowed != 0, scores, NEG_FILL)
    scores = scores.reshape(-1, src, scores.shape[1])
    exp_terms = jnp.exp(scores - jnp.max(scores, axis=1, keepdims=True))
    probs = exp_terms / jnp.sum(exp_terms, axis=1, keepdims=True)
    return probs.reshape(allowed.shape)


def d_scores_of(probs, d_probs, scale, src):
    shape = probs.shape
    probs = probs.reshape(-1, src, shape[1])
    d_probs = d_probs.reshape(probs.shape)
    inner = jnp.sum(probs * d_probs, axis=1, keepdims=True)
    return (probs * (d_probs - inner) * scale).reshape(shape)


def picked(take, came, held):
    return jnp.where(take[0] != 0, came[...], held[...])


def forward_kernel(n, scale, src, take, came, held, allowed, factor, *refs):
    query_folds, out_folds, (current, following) = refs[:n], refs[n : 2 * n], refs[2 * n :]
    tokens = picked(take, came, held)
    current[...] = tokens
    probs = probs_of(query_folds, tokens, allowed[...], scale, src)
    summed = spread(probs, out_folds)
    following[...] = (tokens.astype(F32) + factor[...] * summed).astype(BF)


def backward(probs, grad, factor, query_folds, out_folds, scale, src):
    d_out = (grad.astype(F32) * factor[...]).astype(BF)
    d_scores = d_scores_of(probs, scores_of(out_folds, d_out), scale, src)
    return (grad.astype(F32) + spread(d_scores, query_folds)).astype(BF)


def turn_kernel(n, scale, src, take, came, held, allowed, factor, grad, *refs):
    query_folds, out_folds, (current, kept, before) = refs[:n], refs[n : 2 * n], refs[2 * n :]
    tokens = picked(take, came, held)
    current[...] = tokens
    probs = probs_of(query_folds, tokens, allowed[...], scale, src)
    kept[...] = probs
    before[...] = backward(probs, grad[...], factor, query_folds, out_folds, scale, src)


def backward_kernel(n, scale, src, take, came, held, probs, factor, *refs):
    query_folds, out_folds, (current, before) = refs[:n], refs[n : 2 * n], refs[2 * n :]
    grad = picked(take, came, held)
    current[...] = grad
    before[...] = backward(probs[...], grad, factor, query_folds, out_folds, scale, src)


def on_chip(body, outs, first, *args):
    vmem = pl.BlockSpec(memory_space=pltpu.VMEM)
    size = sum(math.prod(a.shape) * a.dtype.itemsize for a in args)
    flops = 8 * args[0].shape[0] * sum(math.prod(a.shape) for a in args[-8:])
    return pl.pallas_call(
        body,
        out_shape=[jax.ShapeDtypeStruct(*out) for out in outs],
        in_specs=[pl.BlockSpec(memory_space=pltpu.SMEM)] + [vmem] * len(args),
        out_specs=[vmem] * len(outs),
        compiler_params=pltpu.CompilerParams(vmem_limit_bytes=2 * size + 4 * MEBI),
        cost_estimate=pl.CostEstimate(flops=flops, bytes_accessed=size, transcendentals=0),
    )(first, *args)


def per_device(
    memory, decoder_in, cotangent, src_lengths, tgt_segments, seeds, w_query, w_key, w_value, w_out
):
    micro_count, tgt_rows, dim = decoder_in.shape
    local_cols = w_query.shape[2]
    heads = local_cols // HD
    scale = 1.0 / math.sqrt(HD)
    sections = lax.axis_size("section")
    n_mp = lax.axis_size("mp")
    section = lax.axis_index("section")
    me = lax.axis_index("mp")
    share = n_mp // micro_count
    rows = tgt_rows // share
    src = sections * n_mp
    wq, wk, wv, wo = w_query[0], w_key[0], w_value[0], w_out[0]

    over_z = jnp.concatenate(gather_swaps(memory, "section", range(sections)), axis=0)
    over_x = jnp.stack(gather_swaps(over_z, "mp", range(0, n_mp, 2)), axis=1)
    over_core = jnp.stack(gather_swaps(over_x, "mp", range(2)), axis=2)
    mem_rows = over_core.reshape(src, micro_count, dim)

    def row_ids(device):
        a = jnp.arange(sections, dtype=jnp.int32)[:, None]
        j = jnp.arange(n_mp, dtype=jnp.int32)[None, :]
        return ((section ^ a) * n_mp + (device ^ j)).reshape(src)

    doc_ends = jnp.cumsum(src_lengths, axis=1)

    def allowed_of(owner, heads_owner):
        micro = owner // share
        ends = lax.dynamic_index_in_dim(doc_ends, micro, 0, keepdims=False)
        segments = lax.dynamic_index_in_dim(tgt_segments, micro, 0, keepdims=False)
        segments = lax.dynamic_slice_in_dim(segments, (owner % share) * rows, rows, 0)
        ids = row_ids(heads_owner)
        docs = jnp.sum((ends[None, :] <= ids[:, None]).astype(jnp.int32), axis=1)
        return segments[:, None] == docs[None, :]

    keys = dot_f32("rbd,dk->brk", mem_rows, wk).astype(BF)
    values = dot_f32("rbd,dk->brk", mem_rows, wv).astype(BF)

    def by_owner(array):
        return jnp.stack(
            [
                lax.dynamic_index_in_dim(array, (me ^ j) // share, 0, keepdims=False)
                for j in range(n_mp)
            ]
        )

    keys = by_owner(keys).reshape(n_mp, src, heads, HD)
    values = by_owner(values).reshape(n_mp, src, heads, HD)
    out_fold = jnp.stack(
        [
            dot_f32("jsk,kd->jsd", values[:, :, h], wo[h * HD : (h + 1) * HD]).astype(BF)
            for h in range(heads)
        ],
        axis=1,
    )
    query_fold = jnp.stack(
        [
            dot_f32("jsk,dk->jsd", keys[:, :, h], wq[:, h * HD : (h + 1) * HD]).astype(BF)
            for h in range(heads)
        ],
        axis=1,
    )

    def to_owners(fold):
        fold = fold.reshape(n_mp, heads * src, dim)
        return [fold[j] if j == 0 else swap(fold[j], "mp", j) for j in range(n_mp)]

    out_folds = to_owners(out_fold)
    query_folds = to_owners(query_fold)
    allowed = jnp.stack([allowed_of(me, me ^ k).T for k in range(n_mp)])[:, None]
    allowed = jnp.broadcast_to(allowed, (n_mp, heads, src, rows)).astype(jnp.int32)
    allowed = allowed.reshape(n_mp * heads * src, rows)

    my_micro = me // share
    my_first = (me % share) * rows

    def mine(array):
        part = lax.dynamic_index_in_dim(array, my_micro, 0, keepdims=False)
        return lax.dynamic_slice_in_dim(part, my_first, rows, 0)

    factor = keep_factor(seeds[my_micro, 0], my_first, rows, dim)
    folds = (*query_folds, *out_folds)
    wide = ((rows, dim), BF)

    def at(step):
        return (section == step).astype(jnp.int32)[None]

    held = mine(decoder_in)
    factor, held, allowed = lax.optimization_barrier((factor, held, allowed))
    came = held
    for step in range(sections - 1):
        body = functools.partial(forward_kernel, n_mp, scale, src)
        held, following = on_chip(
            body, [wide, wide], at(step), came, held, allowed, factor, *folds
        )
        came = lax.ppermute(following, "section", [(step, step + 1)])
    step = sections - 1
    body = functools.partial(turn_kernel, n_mp, scale, src)
    grad = mine(cotangent)
    current, probs, before = on_chip(
        body, [wide, (allowed.shape, F32), wide], at(step), came, held, allowed, factor, grad, *folds
    )
    body = functools.partial(forward_kernel, n_mp, scale, src)
    _, following = on_chip(
        body, [wide, wide], at(step), current, current, allowed, factor, *folds
    )

    def all_tokens(array):
        over_x = jnp.stack(gather_swaps(array, "mp", range(0, n_mp, 2)))
        return jnp.stack(gather_swaps(over_x, "mp", range(2)), axis=1).reshape(n_mp * rows, dim)

    out_cols = dim // n_mp
    following = following.reshape(rows, n_mp, out_cols)
    blocks = []
    for j in range(n_mp):
        part = lax.dynamic_index_in_dim(following, me ^ j, 1, keepdims=False)
        blocks.append(part if j == 0 else swap(part, "mp", j))
    stacked = jnp.stack(blocks)
    ordered = [
        lax.dynamic_index_in_dim(stacked, me ^ owner, 0, keepdims=False) for owner in range(n_mp)
    ]
    section_out = jnp.stack(ordered).reshape(1, micro_count, tgt_rows, out_cols)

    every_x = all_tokens(current)
    query = jnp.dot(every_x, wq, preferred_element_type=F32).astype(BF)
    query = query.reshape(n_mp, rows, heads, HD)
    own_allowed = jnp.stack([allowed_of(me ^ j, me) for j in range(n_mp)])[:, None]
    own_probs = softmax_rows(dot_f32("jthk,jshk->jhts", query, keys) * scale, own_allowed)

    for step in range(sections - 1, 0, -1):
        came = lax.ppermute(before, "section", [(step, step - 1)])
        if step == 1:
            break
        if step == 2:
            came, section_out, query, own_probs = lax.optimization_barrier(
                (came, section_out, query, own_probs)
            )
        body = functools.partial(backward_kernel, n_mp, scale, src)
        grad, before = on_chip(
            body, [wide, wide], at(step - 1), came, grad, probs, factor, *folds
        )
    grad = jnp.where(section == 0, came, grad)
    d_out = (grad.astype(F32) * factor).astype(BF)

    every_d_out = all_tokens(d_out)
    d_att = dot_f32("td,kd->tk", every_d_out, wo).astype(BF).reshape(n_mp, rows, heads, HD)
    d_probs = dot_f32("jthk,jshk->jhts", d_att, values)
    inner = jnp.sum(own_probs * d_probs, axis=-1, keepdims=True)
    d_scores = (own_probs * (d_probs - inner) * scale).astype(BF)
    d_keys = dot_f32("jhts,jthk->jshk", d_scores, query).reshape(n_mp, src, local_cols)
    d_values = dot_f32("jhts,jthk->jshk", own_probs.astype(BF), d_att)
    d_values = d_values.reshape(n_mp, src, local_cols)

    def by_micro(array):
        parts = []
        for micro in range(micro_count):
            total = 0.0
            for q in range(share):
                owner = me ^ (micro * share + q)
                total = total + lax.dynamic_index_in_dim(array, owner, 0, keepdims=False)
            parts.append(total.astype(BF))
        return jnp.stack(parts, axis=1)

    terms = dot_f32("rbk,dk->rbd", by_micro(d_keys), wk) + dot_f32(
        "rbk,dk->rbd", by_micro(d_values), wv
    )
    terms = terms.reshape(sections, n_mp // 2, 2, micro_count, dim)
    half = terms[:, :, 0] + swap(terms[:, :, 1].astype(BF), "mp", 1).astype(F32)
    total = half[:, 0]
    for j in range(1, n_mp // 2):
        total = total + swap(half[:, j].astype(BF), "mp", 2 * j).astype(F32)
    mem_grad = total[0]
    for a in range(1, sections):
        mem_grad = mem_grad + swap(total[a].astype(BF), "section", a).astype(F32)

    return (section_out, mem_grad[None])


def solution(mesh):
    return jax.shard_map(
        per_device,
        mesh=mesh,
        in_specs=(
            P(("section", "mp"), "groups", None),
            P("groups", None, None),
            P("groups", None, None),
            P("groups", None),
            P("groups", None),
            P("groups", "section"),
            P("section", None, "mp"),
            P("section", None, "mp"),
            P("section", None, "mp"),
            P("section", "mp", None),
        ),
        out_specs=(P("section", "groups", None, "mp"), P(("section", "mp"), "groups", None)),
        check_vma=False,
    )
```

```python
import functools
import math

import jax
import jax.numpy as jnp
from jax import lax
from jax.experimental import pallas as pl
from jax.experimental.pallas import tpu as pltpu
from jax.sharding import PartitionSpec as P

HD = 256
NEG_FILL = -1e30
KEEP_SCALE = 8.0 / 7.0
BF = jnp.bfloat16
F32 = jnp.float32
MEBI = 1024 * 1024
NN = (((1,), (0,)), ((), ()))
NT = (((1,), (1,)), ((), ()))
SCALE = 1.0 / math.sqrt(HD)


def shifted_right(source_bits, amount):
    return lax.shift_right_logical(source_bits, jnp.full(source_bits.shape, amount, jnp.int32))


def keep_factor(seed_value, first_row, row_count, col_count):
    position = (
        (first_row + jnp.arange(row_count, dtype=jnp.int32))[:, None] * col_count
        + jnp.arange(col_count, dtype=jnp.int32)[None, :]
    )
    hashed = position ^ seed_value * 1640531527
    hashed = hashed ^ shifted_right(hashed, 16)
    hashed = hashed * 2146121005
    hashed = hashed ^ shifted_right(hashed, 15)
    hashed = hashed * 1911520717
    hashed = hashed ^ shifted_right(hashed, 16)
    is_kept = shifted_right(hashed, 8) & 7 != 0
    return jnp.where(is_kept, KEEP_SCALE, 0.0).astype(F32)


def swap(array, axis, k):
    size = lax.axis_size(axis)
    return lax.ppermute(array, axis, [(i, i ^ k) for i in range(size)])


def over_mp(array):
    evens = [array]
    for k in range(2, lax.axis_size("mp"), 2):
        evens.append(swap(array, "mp", k))
    pieces = []
    for even in evens:
        pieces += [even, swap(even, "mp", 1)]
    return pieces


def product(left, right, dims):
    return lax.dot_general(left, right, dims, preferred_element_type=F32)


def softmax_down(scores, allowed, src):
    shape = scores.shape
    scores = jnp.where(allowed != 0, scores * SCALE, NEG_FILL).reshape(-1, src, shape[1])
    exp_terms = jnp.exp(scores - jnp.max(scores, axis=1, keepdims=True))
    return (exp_terms / jnp.sum(exp_terms, axis=1, keepdims=True)).reshape(shape)


def softmax_back(probs, d_probs, src):
    shape = probs.shape
    probs = probs.reshape(-1, src, shape[1])
    d_probs = d_probs.reshape(probs.shape)
    inner = jnp.sum(probs * d_probs, axis=1, keepdims=True)
    return (probs * (d_probs - inner) * SCALE).reshape(shape)


def spread(weights, fold):
    return product(jnp.transpose(weights).astype(BF), fold[...], NN)


def picked(where, step, came, held):
    return jnp.where(where[0] == step, came[...], held[...])


def keys_values_kernel(n, src, heads, where, *refs):
    pieces, (by_owner, wk, wv, wo, keys, values), folds = refs[:n], refs[n : n + 6], refs[n + 6 :]
    rows = jnp.concatenate([piece[...] for piece in pieces], axis=0)
    for weight, out in ((wv, values), (wk, keys)):
        flat = product(rows, weight[...], NN).astype(BF)
        out[...] = product(by_owner[...], flat, NN).astype(BF)
    fold_loop(n, src, heads, values, folds, lambda h, cols: wo[h * HD : (h + 1) * HD, cols], NN)


def fold_loop(n, src, heads, source, folds, weight, dims):
    dim = folds[0].shape[1]
    width = min(dim, 1024)
    for first in range(0, dim, width):
        cols = slice(first, first + width)
        for h in range(heads):
            part = product(source[:, h * HD : (h + 1) * HD], weight(h, cols), dims).astype(BF)
            for k in range(n):
                folds[k][h * src : (h + 1) * src, cols] = part[k * src : (k + 1) * src]


def query_fold_kernel(n, src, heads, where, keys, wq, *folds):
    fold_loop(n, src, heads, keys, folds, lambda h, cols: wq[cols, h * HD : (h + 1) * HD], NT)


def forward(tokens, allowed, factor, query_fold, out_fold, src):
    probs = softmax_down(product(query_fold[...], tokens, NT), allowed[...], src)
    return (tokens.astype(F32) + factor[...] * spread(probs, out_fold)).astype(BF)


def first_kernel(n, src, where, held, allowed, factor, *refs):
    blocks, (query_fold, out_fold, following) = refs[: 2 * n], refs[2 * n :]
    size = blocks[0].shape[0]
    for k in range(n):
        query_fold[k * size : (k + 1) * size] = blocks[k][...]
        out_fold[k * size : (k + 1) * size] = blocks[n + k][...]
    following[...] = forward(held[...], allowed, factor, query_fold, out_fold, src)


def forward_kernel(
    step, src, where, came, held, allowed, factor, query_fold, out_fold, current, following
):
    tokens = picked(where, step, came, held)
    current[...] = tokens
    following[...] = forward(tokens, allowed, factor, query_fold, out_fold, src)


def backward(probs, grad, factor, query_fold, out_fold, src):
    d_out = (grad.astype(F32) * factor[...]).astype(BF)
    d_scores = softmax_back(probs, product(out_fold[...], d_out, NT), src)
    return (grad.astype(F32) + spread(d_scores, query_fold)).astype(BF)


def turn_kernel(
    step, src, where, came, held, allowed, factor, query_fold, out_fold, grad, current, kept, before
):
    tokens = picked(where, step, came, held)
    current[...] = tokens
    probs = softmax_down(product(query_fold[...], tokens, NT), allowed[...], src)
    kept[...] = probs
    before[...] = backward(probs, grad[...], factor, query_fold, out_fold, src)


def backward_kernel(
    step, src, where, came, held, probs, factor, query_fold, out_fold, current, before
):
    grad = picked(where, step, came, held)
    current[...] = grad
    before[...] = backward(probs[...], grad, factor, query_fold, out_fold, src)


def dropped_kernel(step, where, came, held, factor, d_out):
    grad = picked(where, step, came, held)
    d_out[...] = (grad.astype(F32) * factor[...]).astype(BF)


def outputs_kernel(n, where, current, probs, factor, out_fold, *parts):
    width = parts[0].shape[1]
    turned = jnp.transpose(probs[...]).astype(BF)
    for j in range(n):
        cols = pl.ds(pl.multiple_of((where[1] ^ j) * width, width), width)
        summed = product(turned, out_fold[:, cols], NN)
        total = current[:, cols].astype(F32) + factor[:, cols] * summed
        parts[j][...] = total.astype(BF)


def order_kernel(n, where, *refs):
    for j in range(n):
        refs[n][where[1] ^ j] = refs[j][...]


def heads_of(n, heads, rows, src):
    for k in range(n):
        for h in range(heads):
            tile = slice((k * heads + h) * src, (k * heads + h + 1) * src)
            cols = slice(h * HD, (h + 1) * HD)
            yield tile, slice(k * rows, (k + 1) * rows), slice(k * src, (k + 1) * src), cols


def query_kernel(n, src, heads, where, keys, wq, allowed, *refs):
    pieces, (query, probs) = refs[:n], refs[n:]
    rows = pieces[0].shape[0]
    tokens = jnp.concatenate([piece[...] for piece in pieces], axis=0)
    query[...] = product(tokens, wq[...], NN).astype(BF)
    for tile, toks, srcs, cols in heads_of(n, heads, rows, src):
        scores = product(keys[srcs, cols], query[toks, cols], NT)
        probs[tile] = softmax_down(scores, allowed[tile], src)


def terms_kernel(n, src, heads, where, keys, values, query, probs, by_micro, wk, wv, wo, *refs):
    pieces, (kept, sent, d_att, d_keys, d_values) = refs[:n], refs[n:]
    rows = pieces[0].shape[0]
    grads = jnp.concatenate([piece[...] for piece in pieces], axis=0)
    d_att[...] = product(grads, wo[...], NT).astype(BF)
    for tile, toks, srcs, cols in heads_of(n, heads, rows, src):
        own = probs[tile]
        d_scores = softmax_back(own, product(values[srcs, cols], d_att[toks, cols], NT), src)
        d_keys[srcs, cols] = product(d_scores.astype(BF), query[toks, cols], NN).astype(BF)
        d_values[srcs, cols] = product(own.astype(BF), d_att[toks, cols], NN).astype(BF)
    key_rows = product(by_micro[...], d_keys[...], NN).astype(BF)
    value_rows = product(by_micro[...], d_values[...], NN).astype(BF)
    size = key_rows.shape[0] // n
    dim = kept.shape[1]
    width = min(dim, 1024)
    for first in range(0, dim, width):
        cols = slice(first, first + width)
        part = product(key_rows, wk[cols], NT) + product(value_rows, wv[cols], NT)
        for k in range(0, n, 2):
            to = slice(k // 2 * size, (k // 2 + 1) * size)
            kept[to, cols] = part[k * size : (k + 1) * size]
            sent[to, cols] = part[(k + 1) * size : (k + 2) * size].astype(BF)


def on_chip(body, outs, where, *args, scratch=()):
    vmem = pl.BlockSpec(memory_space=pltpu.VMEM)
    outs = [jax.ShapeDtypeStruct(*out) for out in outs]
    size = sum(math.prod(a.shape) * a.dtype.itemsize for a in (*args, *outs, *scratch))
    return pl.pallas_call(
        body,
        out_shape=outs,
        in_specs=[pl.BlockSpec(memory_space=pltpu.SMEM)] + [vmem] * len(args),
        out_specs=[vmem] * len(outs),
        scratch_shapes=[pltpu.VMEM(s.shape, s.dtype) for s in scratch],
        compiler_params=pltpu.CompilerParams(vmem_limit_bytes=size + size // 2 + 4 * MEBI),
        cost_estimate=pl.CostEstimate(
            flops=64 * size, bytes_accessed=size, transcendentals=0
        ),
    )(where, *args)


def per_device(
    memory, decoder_in, cotangent, src_lengths, tgt_segments, seeds, w_query, w_key, w_value, w_out
):
    micro_count, tgt_rows, dim = decoder_in.shape
    local_cols = w_query.shape[2]
    heads = local_cols // HD
    sections = lax.axis_size("section")
    n_mp = lax.axis_size("mp")
    section = lax.axis_index("section")
    me = lax.axis_index("mp")
    where = jnp.stack([section, me]).astype(jnp.int32)
    share = n_mp // micro_count
    rows = tgt_rows // share
    src = sections * n_mp
    fold_rows = heads * src
    wq, wk, wv, wo = w_query[0], w_key[0], w_value[0], w_out[0]

    own = memory.reshape(micro_count, dim)
    over_z = [own if a == 0 else swap(own, "section", a) for a in range(sections)]
    pieces = over_mp(jnp.concatenate(over_z, axis=0))

    def row_ids(device):
        j = jnp.arange(n_mp, dtype=jnp.int32)[:, None]
        a = jnp.arange(sections, dtype=jnp.int32)[None, :]
        return ((section ^ a) * n_mp + (device ^ j)).reshape(src)

    doc_ends = jnp.cumsum(src_lengths, axis=1)

    def allowed_of(owner, heads_owner):
        micro = owner // share
        ends = lax.dynamic_index_in_dim(doc_ends, micro, 0, keepdims=False)
        segments = lax.dynamic_index_in_dim(tgt_segments, micro, 0, keepdims=False)
        segments = lax.dynamic_slice_in_dim(segments, (owner % share) * rows, rows, 0)
        docs = jnp.sum((ends[None, :] <= row_ids(heads_owner)[:, None]).astype(jnp.int32), axis=1)
        return docs[:, None] == segments[None, :]

    def every_head(blocks):
        blocks = jnp.broadcast_to(jnp.stack(blocks)[:, None], (n_mp, heads, src, rows))
        return blocks.astype(jnp.int32).reshape(n_mp * fold_rows, rows)

    allowed = every_head([allowed_of(me, me ^ k) for k in range(n_mp)])
    own_allowed = every_head([allowed_of(me ^ j, me) for j in range(n_mp)])

    to_row = jnp.arange(n_mp * src, dtype=jnp.int32)[:, None]
    from_row = jnp.arange(src * micro_count, dtype=jnp.int32)[None, :]
    by_owner = (to_row % src == from_row // micro_count) & (
        (me ^ (to_row // src)) // share == from_row % micro_count
    )
    by_owner = by_owner.astype(BF)

    def mine(array):
        part = lax.dynamic_index_in_dim(array, me // share, 0, keepdims=False)
        return lax.dynamic_slice_in_dim(part, (me % share) * rows, rows, 0)

    factor = keep_factor(seeds[me // share, 0], (me % share) * rows, rows, dim)
    held = mine(decoder_in)
    grad = mine(cotangent)
    allowed, own_allowed, by_owner, by_micro, factor, held, grad = lax.optimization_barrier(
        (allowed, own_allowed, by_owner, by_owner.T, factor, held, grad)
    )

    wide = ((rows, dim), BF)
    stacked = ((n_mp * src, local_cols), BF)
    block = ((fold_rows, dim), BF)
    whole_fold = ((n_mp * fold_rows, dim), BF)
    keys, values, *out_blocks = on_chip(
        functools.partial(keys_values_kernel, n_mp, src, heads),
        [stacked, stacked] + [block] * n_mp,
        where,
        *pieces,
        by_owner,
        wk,
        wv,
        wo,
    )
    query_blocks = on_chip(
        functools.partial(query_fold_kernel, n_mp, src, heads), [block] * n_mp, where, keys, wq
    )

    def to_owners(blocks):
        return [part if j == 0 else swap(part, "mp", j) for j, part in enumerate(blocks)]

    out_blocks = to_owners(out_blocks)
    query_blocks = to_owners(query_blocks)
    query_fold, out_fold, following = on_chip(
        functools.partial(first_kernel, n_mp, src),
        [whole_fold, whole_fold, wide],
        where,
        held,
        allowed,
        factor,
        *query_blocks,
        *out_blocks,
    )
    folds = (query_fold, out_fold)
    for step in range(1, sections):
        came = lax.ppermute(following, "section", [(step - 1, step)])
        if step < sections - 1:
            held, following = on_chip(
                functools.partial(forward_kernel, step, src),
                [wide, wide],
                where,
                came,
                held,
                allowed,
                factor,
                *folds,
            )
    current, probs, before = on_chip(
        functools.partial(turn_kernel, sections - 1, src),
        [wide, (allowed.shape, F32), wide],
        where,
        came,
        held,
        allowed,
        factor,
        *folds,
        grad,
    )

    out_cols = dim // n_mp
    for step in range(sections - 1, 0, -1):
        came = lax.ppermute(before, "section", [(step, step - 1)])
        if step == 3:
            parts = on_chip(
                functools.partial(outputs_kernel, n_mp),
                [((rows, out_cols), BF)] * n_mp,
                where,
                current,
                probs,
                factor,
                out_fold,
            )
            came, parts = lax.optimization_barrier((came, parts))
        if step == 2:
            came, parts = lax.optimization_barrier((came, to_owners(parts)))
        if step == 1:
            (section_out,) = on_chip(
                functools.partial(order_kernel, n_mp),
                [((n_mp, rows, out_cols), BF)],
                where,
                *parts,
            )
            came, section_out, every_x = lax.optimization_barrier(
                (came, section_out, over_mp(current))
            )
            break
        grad, before = on_chip(
            functools.partial(backward_kernel, step - 1, src),
            [wide, wide],
            where,
            came,
            grad,
            probs,
            factor,
            *folds,
        )
    (d_out,) = on_chip(functools.partial(dropped_kernel, 0), [wide], where, came, grad, factor)

    query, own_probs = on_chip(
        functools.partial(query_kernel, n_mp, src, heads),
        [((n_mp * rows, local_cols), BF), (own_allowed.shape, F32)],
        where,
        keys,
        wq,
        own_allowed,
        *every_x,
    )
    half_rows = n_mp // 2 * sections * micro_count
    kept, sent = on_chip(
        functools.partial(terms_kernel, n_mp, src, heads),
        [((half_rows, dim), F32), ((half_rows, dim), BF)],
        where,
        keys,
        values,
        query,
        own_probs,
        by_micro,
        wk,
        wv,
        wo,
        *over_mp(d_out),
        scratch=[
            jax.ShapeDtypeStruct((n_mp * rows, local_cols), BF),
            jax.ShapeDtypeStruct(*stacked),
            jax.ShapeDtypeStruct(*stacked),
        ],
    )
    half = (kept + swap(sent, "mp", 1).astype(F32)).reshape(n_mp // 2, -1, dim)
    total = half[0]
    for j in range(1, n_mp // 2):
        total = total + swap(half[j].astype(BF), "mp", 2 * j).astype(F32)
    total = total.reshape(sections, micro_count, dim)
    mem_grad = total[0]
    for a in range(1, sections):
        mem_grad = mem_grad + swap(total[a].astype(BF), "section", a).astype(F32)
    return (section_out.reshape(1, micro_count, tgt_rows, out_cols), mem_grad[None])


def solution(mesh):
    return jax.shard_map(
        per_device,
        mesh=mesh,
        in_specs=(
            P(("section", "mp"), "groups", None),
            P("groups", None, None),
            P("groups", None, None),
            P("groups", None),
            P("groups", None),
            P("groups", "section"),
            P("section", None, "mp"),
            P("section", None, "mp"),
            P("section", None, "mp"),
            P("section", "mp", None),
        ),
        out_specs=(P("section", "groups", None, "mp"), P(("section", "mp"), "groups", None)),
        check_vma=False,
    )
```

```python
import functools
import math

import jax
import jax.numpy as jnp
from jax import lax
from jax.experimental import pallas as pl
from jax.experimental.pallas import tpu as pltpu
from jax.sharding import PartitionSpec as P

HD = 256
NEG_FILL = -1e30
KEEP_SCALE = 8.0 / 7.0
BF = jnp.bfloat16
F32 = jnp.float32
MEBI = 1024 * 1024
BESIDE_THE_GATHER = 32 * MEBI
NN = (((1,), (0,)), ((), ()))
NT = (((1,), (1,)), ((), ()))
SCALE = 1.0 / math.sqrt(HD)


def shifted_right(source_bits, amount):
    return lax.shift_right_logical(source_bits, jnp.full(source_bits.shape, amount, jnp.int32))


def keep_factor(seed_value, first_row, first_col, shape, col_count):
    rows = first_row + lax.broadcasted_iota(jnp.int32, shape, 0)
    position = rows * col_count + first_col + lax.broadcasted_iota(jnp.int32, shape, 1)
    hashed = position ^ seed_value * 1640531527
    hashed = hashed ^ shifted_right(hashed, 16)
    hashed = hashed * 2146121005
    hashed = hashed ^ shifted_right(hashed, 15)
    hashed = hashed * 1911520717
    hashed = hashed ^ shifted_right(hashed, 16)
    is_kept = shifted_right(hashed, 8) & 7 != 0
    return jnp.where(is_kept, KEEP_SCALE, 0.0).astype(F32)


def prepare_kernel(share, seeds, inputs, cotangent, factor, *refs):
    targets, sems = refs[:-1], refs[-1]
    rows, dim = factor.shape
    chunks = len(targets) // 2
    size = rows // chunks
    owner = lax.axis_index("mp")
    micro = lax.div(owner, share)
    first = pl.multiple_of(lax.rem(owner, share) * rows, rows)
    copies = []
    for k, target in enumerate(targets):
        source = inputs if k < chunks else cotangent
        tokens = pl.ds(first + k % chunks * size, size)
        copies.append(pltpu.make_async_copy(source.at[micro, tokens], target, sems.at[k]))
    for copy in copies:
        copy.start()
    width = min(dim, 512)
    for first_col in range(0, dim, width):
        cols = slice(first_col, first_col + width)
        factor[:, cols] = keep_factor(seeds[micro, 0], first, first_col, (rows, width), dim)
    for copy in copies:
        copy.wait()


def swap(array, axis, k):
    size = lax.axis_size(axis)
    return lax.ppermute(array, axis, [(i, i ^ k) for i in range(size)])


def even_mp(array):
    return [array] + [swap(array, "mp", k) for k in range(2, lax.axis_size("mp"), 2)]


def with_odd_mp(evens):
    pieces = []
    for even in evens:
        pieces += [even, swap(even, "mp", 1)]
    return pieces


def over_mp(array):
    return with_odd_mp(even_mp(array))


def product(left, right, dims):
    return lax.dot_general(left, right, dims, preferred_element_type=F32)


def softmax_down(scores, allowed, src):
    shape = scores.shape
    scores = jnp.where(allowed != 0, scores * SCALE, NEG_FILL).reshape(-1, src, shape[1])
    exp_terms = jnp.exp(scores - jnp.max(scores, axis=1, keepdims=True))
    return (exp_terms / jnp.sum(exp_terms, axis=1, keepdims=True)).reshape(shape)


def softmax_back(probs, d_probs, src):
    shape = probs.shape
    probs = probs.reshape(-1, src, shape[1])
    d_probs = d_probs.reshape(probs.shape)
    inner = jnp.sum(probs * d_probs, axis=1, keepdims=True)
    return (probs * (d_probs - inner) * SCALE).reshape(shape)


def spread(weights, fold):
    return product(jnp.transpose(weights).astype(BF), fold[...], NN)


def picked(step, came, held):
    return jnp.where(lax.axis_index("section") == step, came[...], held[...])


def store_folds(part, h, src, cols, folds):
    for k, fold in enumerate(folds):
        fold[h * src : (h + 1) * src, cols] = part[k * src : (k + 1) * src]


def columns(dim):
    width = min(dim, 1024)
    return [slice(first, first + width) for first in range(0, dim, width)]


def values_kernel(n, src, heads, by_owner, wv, wo, *refs):
    pieces, (values, *folds) = refs[:n], refs[n:]
    rows = jnp.concatenate([piece[...] for piece in pieces], axis=0)
    flat = product(rows, wv[...], NN).astype(BF)
    values[...] = product(by_owner[...], flat, NN).astype(BF)
    for h in range(heads):
        head = slice(h * HD, (h + 1) * HD)
        for cols in columns(wo.shape[1]):
            part = product(values[:, head], wo[head, cols], NN).astype(BF)
            store_folds(part, h, src, cols, folds)


def keys_kernel(n, src, heads, share, by_owner, allowed, inputs, wk, wq, *refs):
    pieces, (keys, *outs) = refs[:n], refs[n : 3 * n + 1]
    folds, probs = outs[:n], outs[n:]
    query = refs[3 * n + 1]
    rows = jnp.concatenate([piece[...] for piece in pieces], axis=0)
    flat = product(rows, wk[...], NN).astype(BF)
    keys[...] = product(by_owner[...], flat, NN).astype(BF)
    me = lax.axis_index("mp")
    count = allowed.shape[1]
    tokens = []
    for j in range(n):
        owner = me ^ j
        first = pl.multiple_of(lax.rem(owner, share) * count, count)
        tokens.append(inputs[lax.div(owner, share), pl.ds(first, count)])
    query[...] = product(jnp.concatenate(tokens, axis=0), wq[...], NN).astype(BF)
    for tile, toks, srcs, cols in heads_of(n, heads, count, src):
        k, h = divmod(tile.start // src, heads)
        own = softmax_down(product(keys[srcs, cols], query[toks, cols], NT), allowed[tile], src)
        probs[k][h * src : (h + 1) * src] = own.astype(BF)
    for h in range(heads):
        head = slice(h * HD, (h + 1) * HD)
        for cols in columns(wq.shape[0]):
            part = product(keys[:, head], wq[cols, head], NT).astype(BF)
            store_folds(part, h, src, cols, folds)


def part_of(array, c, size):
    return array[c * size : (c + 1) * size]


def forward(tokens, allowed, factor, query_fold, out_fold, src):
    probs = softmax_down(product(query_fold[...], tokens, NT), allowed[...], src)
    return (tokens.astype(F32) + factor * spread(probs, out_fold)).astype(BF)


def pack(blocks, fold):
    size = blocks[0].shape[0]
    for k, block in enumerate(blocks):
        fold[k * size : (k + 1) * size] = block[...]


def first_kernel(n, chunks, factor, *refs):
    helds, probs, refs = refs[:chunks], refs[chunks : n + chunks], refs[n + chunks :]
    blocks, (out_fold, *following) = refs[:n], refs[n:]
    pack(blocks, out_fold)
    weights = jnp.concatenate([block[...] for block in probs], axis=0).astype(F32)
    kept = factor[...] * spread(weights, out_fold)
    size = kept.shape[0] // chunks
    for c in range(chunks):
        total = helds[c][...].astype(F32) + kept[c * size : (c + 1) * size]
        following[c][...] = total.astype(BF)


def pack_kernel(n, *refs):
    pack(refs[:n], refs[n])


def forward_kernel(
    step, c, src, came, held, allowed, factor, query_fold, out_fold, current, following
):
    tokens = picked(step, came, held)
    current[...] = tokens
    factor = part_of(factor, c, tokens.shape[0])
    following[...] = forward(tokens, allowed, factor, query_fold, out_fold, src)


def backward(probs, grad, factor, query_fold, out_fold, src):
    d_out = (grad.astype(F32) * factor).astype(BF)
    d_scores = softmax_back(probs, product(out_fold[...], d_out, NT), src)
    return (grad.astype(F32) + spread(d_scores, query_fold)).astype(BF)


def turn_kernel(
    step, c, src, came, held, allowed, factor, query_fold, out_fold, grad, current, kept, before
):
    tokens = picked(step, came, held)
    current[...] = tokens
    probs = softmax_down(product(query_fold[...], tokens, NT), allowed[...], src)
    kept[...] = probs
    factor = part_of(factor, c, tokens.shape[0])
    before[...] = backward(probs, grad[...], factor, query_fold, out_fold, src)


def backward_kernel(
    step, c, src, came, held, probs, factor, query_fold, out_fold, current, before
):
    grad = picked(step, came, held)
    current[...] = grad
    factor = part_of(factor, c, grad.shape[0])
    before[...] = backward(probs[...], grad, factor, query_fold, out_fold, src)


def dropped_kernel(step, c, came, held, factor, d_out):
    grad = picked(step, came, held)
    d_out[...] = (grad.astype(F32) * part_of(factor, c, grad.shape[0])).astype(BF)


def outputs_kernel(n, chunks, factor, out_fold, *refs):
    currents, probs, (whole, *parts) = refs[:chunks], refs[chunks : 2 * chunks], refs[2 * chunks :]
    width = parts[0].shape[1]
    size = currents[0].shape[0]
    turned = [jnp.transpose(block[...]).astype(BF) for block in probs]
    turned = jnp.concatenate(turned, axis=0)
    for c in range(chunks):
        whole[c * size : (c + 1) * size] = currents[c][...]
    for j in range(n):
        cols = pl.ds(pl.multiple_of((lax.axis_index("mp") ^ j) * width, width), width)
        summed = product(turned, out_fold[:, cols], NN)
        total = whole[:, cols].astype(F32) + factor[:, cols] * summed
        parts[j][...] = total.astype(BF)


def order_kernel(n, *refs):
    for j in range(n):
        refs[n][lax.axis_index("mp") ^ j] = refs[j][...]


def heads_of(n, heads, rows, src):
    for k in range(n):
        for h in range(heads):
            tile = slice((k * heads + h) * src, (k * heads + h + 1) * src)
            cols = slice(h * HD, (h + 1) * HD)
            yield tile, slice(k * rows, (k + 1) * rows), slice(k * src, (k + 1) * src), cols


def query_kernel(n, src, heads, keys, wq, allowed, *refs):
    pieces, (query, probs) = refs[:n], refs[n:]
    rows = pieces[0].shape[0]
    tokens = jnp.concatenate([piece[...] for piece in pieces], axis=0)
    query[...] = product(tokens, wq[...], NN).astype(BF)
    for tile, toks, srcs, cols in heads_of(n, heads, rows, src):
        scores = product(keys[srcs, cols], query[toks, cols], NT)
        probs[tile] = softmax_down(scores, allowed[tile], src)


def terms_kernel(n, src, heads, keys, values, query, probs, by_micro, wk, wv, wo, *refs):
    pieces, (kept, sent, d_att, d_keys, d_values) = refs[:-5], refs[-5:]
    rows = query.shape[0] // n
    grads = jnp.concatenate([piece[...] for piece in pieces], axis=0)
    d_att[...] = product(grads, wo[...], NT).astype(BF)
    for tile, toks, srcs, cols in heads_of(n, heads, rows, src):
        own = probs[tile]
        d_scores = softmax_back(own, product(values[srcs, cols], d_att[toks, cols], NT), src)
        d_keys[srcs, cols] = product(d_scores.astype(BF), query[toks, cols], NN).astype(BF)
        d_values[srcs, cols] = product(own.astype(BF), d_att[toks, cols], NN).astype(BF)
    key_rows = product(by_micro[...], d_keys[...], NN).astype(BF)
    value_rows = product(by_micro[...], d_values[...], NN).astype(BF)
    size = key_rows.shape[0] // n
    dim = kept.shape[1]
    width = min(dim, 1024)
    for first in range(0, dim, width):
        cols = slice(first, first + width)
        part = product(key_rows, wk[cols], NT) + product(value_rows, wv[cols], NT)
        for k in range(0, n, 2):
            to = slice(k // 2 * size, (k // 2 + 1) * size)
            kept[to, cols] = part[k * size : (k + 1) * size]
            sent[to, cols] = part[(k + 1) * size : (k + 2) * size].astype(BF)


def on_chip(body, outs, *args, scratch=()):
    vmem = pl.BlockSpec(memory_space=pltpu.VMEM)
    outs = [jax.ShapeDtypeStruct(*out) for out in outs]
    size = sum(math.prod(a.shape) * a.dtype.itemsize for a in (*args, *outs, *scratch))
    return pl.pallas_call(
        body,
        out_shape=outs,
        in_specs=[vmem] * len(args),
        out_specs=[vmem] * len(outs),
        scratch_shapes=[pltpu.VMEM(s.shape, s.dtype) for s in scratch],
        compiler_params=pltpu.CompilerParams(vmem_limit_bytes=size + size // 2 + 4 * MEBI),
        cost_estimate=pl.CostEstimate(
            flops=64 * size, bytes_accessed=size, transcendentals=0
        ),
    )(*args)


def per_device(
    memory, decoder_in, cotangent, src_lengths, tgt_segments, seeds, w_query, w_key, w_value, w_out
):
    micro_count, tgt_rows, dim = decoder_in.shape
    local_cols = w_query.shape[2]
    heads = local_cols // HD
    sections = lax.axis_size("section")
    n_mp = lax.axis_size("mp")
    section = lax.axis_index("section")
    me = lax.axis_index("mp")
    share = n_mp // micro_count
    rows = tgt_rows // share
    src = sections * n_mp
    fold_rows = heads * src
    wq, wk, wv, wo = w_query[0], w_key[0], w_value[0], w_out[0]

    chunks = 2 if rows % 32 == 0 else 1
    wide = ((rows // chunks, dim), BF)
    anywhere = pl.BlockSpec(memory_space=pl.ANY)
    vmem = pl.BlockSpec(memory_space=pltpu.VMEM)
    factor, *tokens = pl.pallas_call(
        functools.partial(prepare_kernel, share),
        out_shape=[jax.ShapeDtypeStruct((rows, dim), F32)]
        + [jax.ShapeDtypeStruct(*wide)] * (2 * chunks),
        in_specs=[pl.BlockSpec(memory_space=pltpu.SMEM), anywhere, anywhere],
        out_specs=[vmem] * (1 + 2 * chunks),
        scratch_shapes=[pltpu.SemaphoreType.DMA((2 * chunks,))],
        compiler_params=pltpu.CompilerParams(vmem_limit_bytes=4 * MEBI),
        cost_estimate=pl.CostEstimate(
            flops=0, bytes_accessed=BESIDE_THE_GATHER, transcendentals=0
        ),
    )(seeds, decoder_in, cotangent)

    own = memory.reshape(micro_count, dim)
    over_z = [own if a == 0 else swap(own, "section", a) for a in range(sections)]
    over_z = jnp.concatenate(over_z, axis=0)
    over_z, factor, tokens = lax.optimization_barrier((over_z, factor, tokens))
    helds, grads = list(tokens[:chunks]), list(tokens[chunks:])
    pieces = over_mp(over_z)

    to_row = jnp.arange(n_mp * src, dtype=jnp.int32)[:, None]
    from_row = jnp.arange(src * micro_count, dtype=jnp.int32)[None, :]
    by_owner = (to_row % src == from_row // micro_count) & (
        (me ^ (to_row // src)) // share == from_row % micro_count
    )
    by_owner = by_owner.astype(BF)

    stacked = ((n_mp * src, local_cols), BF)
    block = ((fold_rows, dim), BF)
    whole_fold = ((n_mp * fold_rows, dim), BF)
    def row_ids(device):
        j = jnp.arange(n_mp, dtype=jnp.int32)[:, None]
        a = jnp.arange(sections, dtype=jnp.int32)[None, :]
        return ((section ^ a) * n_mp + (device ^ j)).reshape(src)

    doc_ends = jnp.cumsum(src_lengths, axis=1)

    def allowed_of(owner, heads_owner):
        micro = owner // share
        ends = lax.dynamic_index_in_dim(doc_ends, micro, 0, keepdims=False)
        segments = lax.dynamic_index_in_dim(tgt_segments, micro, 0, keepdims=False)
        segments = lax.dynamic_slice_in_dim(segments, (owner % share) * rows, rows, 0)
        docs = jnp.sum((ends[None, :] <= row_ids(heads_owner)[:, None]).astype(jnp.int32), axis=1)
        return docs[:, None] == segments[None, :]

    def every_head(blocks):
        blocks = jnp.broadcast_to(jnp.stack(blocks)[:, None], (n_mp, heads, src, rows))
        return blocks.astype(jnp.int32).reshape(n_mp * fold_rows, rows)

    own_allowed = every_head([allowed_of(me ^ j, me) for j in range(n_mp)])
    allowed = every_head([allowed_of(me, me ^ k) for k in range(n_mp)])
    size = rows // chunks
    masks = [lax.slice_in_dim(allowed, c * size, (c + 1) * size, axis=1) for c in range(chunks)]
    own_allowed, by_owner, by_micro, masks = lax.optimization_barrier(
        (own_allowed, by_owner, by_owner.T, masks)
    )
    values, *out_blocks = on_chip(
        functools.partial(values_kernel, n_mp, src, heads),
        [stacked] + [block] * n_mp,
        by_owner,
        wv,
        wo,
        *pieces,
    )
    keys, *blocks = on_chip(
        functools.partial(keys_kernel, n_mp, src, heads, share),
        [stacked] + [block] * n_mp + [((fold_rows, rows), BF)] * n_mp,
        by_owner,
        own_allowed,
        decoder_in,
        wk,
        wq,
        *pieces,
        scratch=[jax.ShapeDtypeStruct((n_mp * rows, local_cols), BF)],
    )
    query_blocks, own_probs = blocks[:n_mp], blocks[n_mp:]
    def to_owners(blocks):
        return [part if j == 0 else swap(part, "mp", j) for j, part in enumerate(blocks)]

    out_blocks = to_owners(out_blocks)
    first_probs = to_owners(own_probs)
    query_blocks = to_owners(query_blocks)
    out_fold, *followings = on_chip(
        functools.partial(first_kernel, n_mp, chunks),
        [whole_fold] + [wide] * chunks,
        factor,
        *helds,
        *first_probs,
        *out_blocks,
    )
    (query_fold,) = on_chip(
        functools.partial(pack_kernel, n_mp), [whole_fold], *query_blocks
    )
    folds = (query_fold, out_fold)
    for step in range(1, sections):
        cames = [lax.ppermute(part, "section", [(step - 1, step)]) for part in followings]
        if step < sections - 1:
            for c in range(chunks):
                helds[c], followings[c] = on_chip(
                    functools.partial(forward_kernel, step, c, src),
                    [wide, wide],
                                cames[c],
                    helds[c],
                    masks[c],
                    factor,
                    *folds,
                )
    currents, probs, befores = [], [], []
    for c in range(chunks):
        results = on_chip(
            functools.partial(turn_kernel, sections - 1, c, src),
            [wide, (masks[c].shape, F32), wide],
                cames[c],
            helds[c],
            masks[c],
            factor,
            *folds,
            grads[c],
        )
        for kept, result in zip((currents, probs, befores), results, strict=True):
            kept.append(result)

    out_cols = dim // n_mp
    for step in range(sections - 1, 0, -1):
        cames = [lax.ppermute(part, "section", [(step, step - 1)]) for part in befores]
        if step == 3:
            whole, *parts = on_chip(
                functools.partial(outputs_kernel, n_mp, chunks),
                [((rows, dim), BF)] + [((rows, out_cols), BF)] * n_mp,
                        factor,
                out_fold,
                *currents,
                *probs,
            )
            cames, whole, parts = lax.optimization_barrier((cames, whole, parts))
        if step == 2:
            cames, parts, evens = lax.optimization_barrier(
                (cames, to_owners(parts), even_mp(whole))
            )
        if step == 1:
            (section_out,) = on_chip(
                functools.partial(order_kernel, n_mp),
                [((n_mp, rows, out_cols), BF)],
                        *parts,
            )
            query, own_probs = on_chip(
                functools.partial(query_kernel, n_mp, src, heads),
                [((n_mp * rows, local_cols), BF), (own_allowed.shape, F32)],
                        keys,
                wq,
                own_allowed,
                *with_odd_mp(evens),
            )
            cames, section_out, query, own_probs = lax.optimization_barrier(
                (cames, section_out, query, own_probs)
            )
            break
        for c in range(chunks):
            grads[c], befores[c] = on_chip(
                functools.partial(backward_kernel, step - 1, c, src),
                [wide, wide],
                        cames[c],
                grads[c],
                probs[c],
                factor,
                *folds,
            )
    gathered = []
    for c in range(chunks):
        (d_out,) = on_chip(
            functools.partial(dropped_kernel, 0, c), [wide], cames[c], grads[c], factor
        )
        gathered.append(over_mp(d_out))
    every_d_out = [gathered[c][j] for j in range(n_mp) for c in range(chunks)]
    half_rows = n_mp // 2 * sections * micro_count
    kept, sent = on_chip(
        functools.partial(terms_kernel, n_mp, src, heads),
        [((half_rows, dim), F32), ((half_rows, dim), BF)],
        keys,
        values,
        query,
        own_probs,
        by_micro,
        wk,
        wv,
        wo,
        *every_d_out,
        scratch=[
            jax.ShapeDtypeStruct((n_mp * rows, local_cols), BF),
            jax.ShapeDtypeStruct(*stacked),
            jax.ShapeDtypeStruct(*stacked),
        ],
    )
    half = (kept + swap(sent, "mp", 1).astype(F32)).reshape(n_mp // 2, -1, dim)
    total = half[0]
    for j in range(1, n_mp // 2):
        total = total + swap(half[j].astype(BF), "mp", 2 * j).astype(F32)
    total = total.reshape(sections, micro_count, dim)
    mem_grad = total[0]
    for a in range(1, sections):
        mem_grad = mem_grad + swap(total[a].astype(BF), "section", a).astype(F32)
    return (section_out.reshape(1, micro_count, tgt_rows, out_cols), mem_grad[None])


def solution(mesh):
    return jax.shard_map(
        per_device,
        mesh=mesh,
        in_specs=(
            P(("section", "mp"), "groups", None),
            P("groups", None, None),
            P("groups", None, None),
            P("groups", None),
            P("groups", None),
            P("groups", "section"),
            P("section", None, "mp"),
            P("section", None, "mp"),
            P("section", None, "mp"),
            P("section", "mp", None),
        ),
        out_specs=(P("section", "groups", None, "mp"), P(("section", "mp"), "groups", None)),
        check_vma=False,
    )
```

```python
import functools
import math

import jax
import jax.numpy as jnp
from jax import lax
from jax.experimental import pallas as pl
from jax.experimental.pallas import tpu as pltpu
from jax.sharding import PartitionSpec as P

HD = 256
NEG_FILL = -1e30
KEEP_SCALE = 8.0 / 7.0
BF = jnp.bfloat16
F32 = jnp.float32
MEBI = 1024 * 1024
LIGHT = pl.CostEstimate(flops=1, bytes_accessed=1, transcendentals=0)
NN = (((1,), (0,)), ((), ()))
NT = (((1,), (1,)), ((), ()))
SCALE = 1.0 / math.sqrt(HD)


def shifted_right(source_bits, amount):
    return lax.shift_right_logical(source_bits, jnp.full(source_bits.shape, amount, jnp.int32))


def keep_factor(seed_value, first_row, first_col, shape, col_count):
    rows = first_row + lax.broadcasted_iota(jnp.int32, shape, 0)
    position = rows * col_count + first_col + lax.broadcasted_iota(jnp.int32, shape, 1)
    hashed = position ^ seed_value * 1640531527
    hashed = hashed ^ shifted_right(hashed, 16)
    hashed = hashed * 2146121005
    hashed = hashed ^ shifted_right(hashed, 15)
    hashed = hashed * 1911520717
    hashed = hashed ^ shifted_right(hashed, 16)
    is_kept = shifted_right(hashed, 8) & 7 != 0
    return jnp.where(is_kept, KEEP_SCALE, 0.0).astype(F32)


def factor_kernel(share, seeds, factor):
    rows, dim = factor.shape
    owner = lax.axis_index("mp")
    seed = seeds[lax.div(owner, share), 0]
    first = lax.rem(owner, share) * rows
    width = min(dim, 512)
    for first_col in range(0, dim, width):
        cols = slice(first_col, first_col + width)
        factor[:, cols] = keep_factor(seed, first, first_col, (rows, width), dim)


def tokens_of(owner, share, array, first, count):
    rows = array.shape[1] // share
    first = pl.multiple_of(lax.rem(owner, share) * rows + first, count)
    return array[lax.div(owner, share), pl.ds(first, count)]


def swap(array, axis, k):
    size = lax.axis_size(axis)
    return lax.ppermute(array, axis, [(i, i ^ k) for i in range(size)])


def even_mp(array):
    return [array] + [swap(array, "mp", k) for k in range(2, lax.axis_size("mp"), 2)]


def with_odd_mp(evens):
    pieces = []
    for even in evens:
        pieces += [even, swap(even, "mp", 1)]
    return pieces


def over_mp(array):
    return with_odd_mp(even_mp(array))


def product(left, right, dims):
    return lax.dot_general(left, right, dims, preferred_element_type=F32)


def softmax_down(scores, allowed, src):
    shape = scores.shape
    scores = jnp.where(allowed != 0, scores * SCALE, NEG_FILL).reshape(-1, src, shape[1])
    exp_terms = jnp.exp(scores - jnp.max(scores, axis=1, keepdims=True))
    return (exp_terms / jnp.sum(exp_terms, axis=1, keepdims=True)).reshape(shape)


def softmax_back(probs, d_probs, src):
    shape = probs.shape
    probs = probs.reshape(-1, src, shape[1])
    d_probs = d_probs.reshape(probs.shape)
    inner = jnp.sum(probs * d_probs, axis=1, keepdims=True)
    return (probs * (d_probs - inner) * SCALE).reshape(shape)


def spread(weights, fold):
    return product(jnp.transpose(weights).astype(BF), fold[...], NN)


def picked(step, came, held):
    return jnp.where(lax.axis_index("section") == step, came[...], held[...])


def here_kernel(n, *refs):
    pass


def on_hand(*arrays):
    vmem = pl.BlockSpec(memory_space=pltpu.VMEM)
    size = sum(math.prod(a.shape) * a.dtype.itemsize for a in arrays)
    return pl.pallas_call(
        functools.partial(here_kernel, len(arrays)),
        out_shape=[jax.ShapeDtypeStruct(a.shape, a.dtype) for a in arrays],
        in_specs=[vmem] * len(arrays),
        out_specs=[vmem] * len(arrays),
        input_output_aliases={k: k for k in range(len(arrays))},
        compiler_params=pltpu.CompilerParams(vmem_limit_bytes=size + 2 * MEBI),
    )(*arrays)


def store_folds(part, h, src, cols, folds):
    for k, fold in enumerate(folds):
        fold[h * src : (h + 1) * src, cols] = part[k * src : (k + 1) * src]


def columns(dim):
    width = min(dim, 1024)
    return [slice(first, first + width) for first in range(0, dim, width)]


def values_kernel(n, src, heads, by_owner, wv, wo, *refs):
    pieces, (values, *folds) = refs[:n], refs[n:]
    rows = jnp.concatenate([piece[...] for piece in pieces], axis=0)
    flat = product(rows, wv[...], NN).astype(BF)
    values[...] = product(by_owner[...], flat, NN).astype(BF)
    for h in range(heads):
        head = slice(h * HD, (h + 1) * HD)
        for cols in columns(wo.shape[1]):
            part = product(values[:, head], wo[head, cols], NN).astype(BF)
            store_folds(part, h, src, cols, folds)


def keys_kernel(n, src, heads, share, by_owner, allowed, inputs, wk, wq, *refs):
    pieces, (keys, *outs) = refs[:n], refs[n : 3 * n + 1]
    folds, probs = outs[:n], outs[n:]
    query = refs[3 * n + 1]
    rows = jnp.concatenate([piece[...] for piece in pieces], axis=0)
    flat = product(rows, wk[...], NN).astype(BF)
    keys[...] = product(by_owner[...], flat, NN).astype(BF)
    me = lax.axis_index("mp")
    count = allowed.shape[1]
    tokens = []
    for j in range(n):
        tokens.append(tokens_of(me ^ j, share, inputs, 0, count))
    query[...] = product(jnp.concatenate(tokens, axis=0), wq[...], NN).astype(BF)
    for tile, toks, srcs, cols in heads_of(n, heads, count, src):
        k, h = divmod(tile.start // src, heads)
        own = softmax_down(product(keys[srcs, cols], query[toks, cols], NT), allowed[tile], src)
        probs[k][h * src : (h + 1) * src] = own.astype(BF)
    for h in range(heads):
        head = slice(h * HD, (h + 1) * HD)
        for cols in columns(wq.shape[0]):
            part = product(keys[:, head], wq[cols, head], NT).astype(BF)
            store_folds(part, h, src, cols, folds)


def part_of(array, c, size):
    return array[c * size : (c + 1) * size]


def forward(tokens, allowed, factor, query_fold, out_fold, src):
    probs = softmax_down(product(query_fold[...], tokens, NT), allowed[...], src)
    return (tokens.astype(F32) + factor * spread(probs, out_fold)).astype(BF)


def pack(blocks, fold):
    size = blocks[0].shape[0]
    for k, block in enumerate(blocks):
        fold[k * size : (k + 1) * size] = block[...]


def first_kernel(n, chunks, share, factor, inputs, *refs):
    probs, blocks, (out_fold, *outs) = refs[:n], refs[n : 2 * n], refs[2 * n :]
    helds, following = outs[:chunks], outs[chunks:]
    pack(blocks, out_fold)
    weights = jnp.concatenate([block[...] for block in probs], axis=0).astype(F32)
    kept = factor[...] * spread(weights, out_fold)
    size = kept.shape[0] // chunks
    for c in range(chunks):
        held = tokens_of(lax.axis_index("mp"), share, inputs, c * size, size)
        helds[c][...] = held
        following[c][...] = (held.astype(F32) + kept[c * size : (c + 1) * size]).astype(BF)


def pack_kernel(n, *refs):
    pack(refs[:n], refs[n])


def forward_kernel(
    step, c, src, came, held, allowed, factor, query_fold, out_fold, current, following
):
    tokens = picked(step, came, held)
    current[...] = tokens
    factor = part_of(factor, c, tokens.shape[0])
    following[...] = forward(tokens, allowed, factor, query_fold, out_fold, src)


def backward(probs, grad, factor, query_fold, out_fold, src):
    d_out = (grad.astype(F32) * factor).astype(BF)
    d_scores = softmax_back(probs, product(out_fold[...], d_out, NT), src)
    return (grad.astype(F32) + spread(d_scores, query_fold)).astype(BF)


def turn_kernel(
    step, c, src, share, came, held, allowed, factor, query_fold, out_fold, cotangent, current, kept, grad, before
):
    tokens = picked(step, came, held)
    current[...] = tokens
    probs = softmax_down(product(query_fold[...], tokens, NT), allowed[...], src)
    kept[...] = probs
    factor = part_of(factor, c, tokens.shape[0])
    grad[...] = tokens_of(lax.axis_index("mp"), share, cotangent, c * tokens.shape[0], tokens.shape[0])
    before[...] = backward(probs, grad[...], factor, query_fold, out_fold, src)


def backward_kernel(
    step, c, src, came, held, probs, factor, query_fold, out_fold, current, before
):
    grad = picked(step, came, held)
    current[...] = grad
    factor = part_of(factor, c, grad.shape[0])
    before[...] = backward(probs[...], grad, factor, query_fold, out_fold, src)


def dropped_kernel(step, c, came, held, factor, d_out):
    grad = picked(step, came, held)
    d_out[...] = (grad.astype(F32) * part_of(factor, c, grad.shape[0])).astype(BF)


def outputs_kernel(n, chunks, factor, out_fold, *refs):
    currents, probs, (whole, *parts) = refs[:chunks], refs[chunks : 2 * chunks], refs[2 * chunks :]
    width = parts[0].shape[1]
    size = currents[0].shape[0]
    turned = [jnp.transpose(block[...]).astype(BF) for block in probs]
    turned = jnp.concatenate(turned, axis=0)
    for c in range(chunks):
        whole[c * size : (c + 1) * size] = currents[c][...]
    for j in range(n):
        cols = pl.ds(pl.multiple_of((lax.axis_index("mp") ^ j) * width, width), width)
        summed = product(turned, out_fold[:, cols], NN)
        total = whole[:, cols].astype(F32) + factor[:, cols] * summed
        parts[j][...] = total.astype(BF)


def order_kernel(n, *refs):
    for j in range(n):
        refs[n][lax.axis_index("mp") ^ j] = refs[j][...]


def heads_of(n, heads, rows, src):
    for k in range(n):
        for h in range(heads):
            tile = slice((k * heads + h) * src, (k * heads + h + 1) * src)
            cols = slice(h * HD, (h + 1) * HD)
            yield tile, slice(k * rows, (k + 1) * rows), slice(k * src, (k + 1) * src), cols


def query_kernel(n, src, heads, keys, wq, allowed, *refs):
    pieces, (query, probs) = refs[:n], refs[n:]
    rows = pieces[0].shape[0]
    tokens = jnp.concatenate([piece[...] for piece in pieces], axis=0)
    query[...] = product(tokens, wq[...], NN).astype(BF)
    for tile, toks, srcs, cols in heads_of(n, heads, rows, src):
        scores = product(keys[srcs, cols], query[toks, cols], NT)
        probs[tile] = softmax_down(scores, allowed[tile], src)


def terms_kernel(n, src, heads, keys, values, query, probs, by_micro, wk, wv, wo, *refs):
    pieces, (kept, sent, d_att, d_keys, d_values) = refs[:-5], refs[-5:]
    rows = query.shape[0] // n
    grads = jnp.concatenate([piece[...] for piece in pieces], axis=0)
    d_att[...] = product(grads, wo[...], NT).astype(BF)
    for tile, toks, srcs, cols in heads_of(n, heads, rows, src):
        own = probs[tile]
        d_scores = softmax_back(own, product(values[srcs, cols], d_att[toks, cols], NT), src)
        d_keys[srcs, cols] = product(d_scores.astype(BF), query[toks, cols], NN).astype(BF)
        d_values[srcs, cols] = product(own.astype(BF), d_att[toks, cols], NN).astype(BF)
    key_rows = product(by_micro[...], d_keys[...], NN).astype(BF)
    value_rows = product(by_micro[...], d_values[...], NN).astype(BF)
    size = key_rows.shape[0] // n
    dim = kept.shape[1]
    width = min(dim, 1024)
    for first in range(0, dim, width):
        cols = slice(first, first + width)
        part = product(key_rows, wk[cols], NT) + product(value_rows, wv[cols], NT)
        for k in range(0, n, 2):
            to = slice(k // 2 * size, (k // 2 + 1) * size)
            kept[to, cols] = part[k * size : (k + 1) * size]
            sent[to, cols] = part[(k + 1) * size : (k + 2) * size].astype(BF)


def on_chip(body, outs, *args, scratch=()):
    vmem = pl.BlockSpec(memory_space=pltpu.VMEM)
    outs = [jax.ShapeDtypeStruct(*out) for out in outs]
    size = sum(math.prod(a.shape) * a.dtype.itemsize for a in (*args, *outs, *scratch))
    return pl.pallas_call(
        body,
        out_shape=outs,
        in_specs=[vmem] * len(args),
        out_specs=[vmem] * len(outs),
        scratch_shapes=[pltpu.VMEM(s.shape, s.dtype) for s in scratch],
        compiler_params=pltpu.CompilerParams(vmem_limit_bytes=size + 3 * MEBI),
        cost_estimate=pl.CostEstimate(flops=64 * size, bytes_accessed=size, transcendentals=0),
    )(*args)


def per_device(
    memory, decoder_in, cotangent, src_lengths, tgt_segments, seeds, w_query, w_key, w_value, w_out
):
    micro_count, tgt_rows, dim = decoder_in.shape
    local_cols = w_query.shape[2]
    heads = local_cols // HD
    sections = lax.axis_size("section")
    n_mp = lax.axis_size("mp")
    section = lax.axis_index("section")
    me = lax.axis_index("mp")
    share = n_mp // micro_count
    rows = tgt_rows // share
    src = sections * n_mp
    fold_rows = heads * src
    wq, wk, wv, wo = w_query[0], w_key[0], w_value[0], w_out[0]

    chunks = 2 if rows % 32 == 0 else 1
    wide = ((rows // chunks, dim), BF)

    own = memory.reshape(micro_count, dim)
    over_z = [own if a == 0 else swap(own, "section", a) for a in range(sections)]
    over_z = jnp.concatenate(over_z, axis=0)
    factor = pl.pallas_call(
        functools.partial(factor_kernel, share),
        out_shape=jax.ShapeDtypeStruct((rows, dim), F32),
        in_specs=[pl.BlockSpec(memory_space=pltpu.SMEM)],
        out_specs=pl.BlockSpec(memory_space=pltpu.VMEM),
        compiler_params=pltpu.CompilerParams(vmem_limit_bytes=4 * MEBI),
        cost_estimate=LIGHT,
    )(seeds)
    over_z, factor, wv_near, wo_near = lax.optimization_barrier(
        (over_z, factor, *on_hand(wv, wo))
    )
    pieces = over_mp(over_z)

    to_row = jnp.arange(n_mp * src, dtype=jnp.int32)[:, None]
    from_row = jnp.arange(src * micro_count, dtype=jnp.int32)[None, :]
    by_owner = (to_row % src == from_row // micro_count) & (
        (me ^ (to_row // src)) // share == from_row % micro_count
    )
    by_owner = by_owner.astype(BF)

    stacked = ((n_mp * src, local_cols), BF)
    block = ((fold_rows, dim), BF)
    whole_fold = ((n_mp * fold_rows, dim), BF)
    def row_ids(device):
        j = jnp.arange(n_mp, dtype=jnp.int32)[:, None]
        a = jnp.arange(sections, dtype=jnp.int32)[None, :]
        return ((section ^ a) * n_mp + (device ^ j)).reshape(src)

    doc_ends = jnp.cumsum(src_lengths, axis=1)

    def allowed_of(owner, heads_owner):
        micro = owner // share
        ends = lax.dynamic_index_in_dim(doc_ends, micro, 0, keepdims=False)
        segments = lax.dynamic_index_in_dim(tgt_segments, micro, 0, keepdims=False)
        segments = lax.dynamic_slice_in_dim(segments, (owner % share) * rows, rows, 0)
        docs = jnp.sum((ends[None, :] <= row_ids(heads_owner)[:, None]).astype(jnp.int32), axis=1)
        return docs[:, None] == segments[None, :]

    def every_head(blocks):
        blocks = jnp.broadcast_to(jnp.stack(blocks)[:, None], (n_mp, heads, src, rows))
        return blocks.astype(jnp.int32).reshape(n_mp * fold_rows, rows)

    own_allowed = every_head([allowed_of(me ^ j, me) for j in range(n_mp)])
    allowed = every_head([allowed_of(me, me ^ k) for k in range(n_mp)])
    size = rows // chunks
    masks = [lax.slice_in_dim(allowed, c * size, (c + 1) * size, axis=1) for c in range(chunks)]
    own_allowed, by_owner, by_micro, masks = lax.optimization_barrier(
        (own_allowed, by_owner, by_owner.T, masks)
    )
    values, *out_blocks = on_chip(
        functools.partial(values_kernel, n_mp, src, heads),
        [stacked] + [block] * n_mp,
        by_owner,
        wv_near,
        wo_near,
        *pieces,
    )
    def to_owners(blocks):
        return [part if j == 0 else swap(part, "mp", j) for j, part in enumerate(blocks)]

    out_blocks = to_owners(out_blocks)
    out_blocks[1], pieces = lax.optimization_barrier((out_blocks[1], pieces))
    keys, *blocks = on_chip(
        functools.partial(keys_kernel, n_mp, src, heads, share),
        [stacked] + [block] * n_mp + [((fold_rows, rows), BF)] * n_mp,
        by_owner,
        own_allowed,
        decoder_in,
        wk,
        wq,
        *pieces,
        scratch=[jax.ShapeDtypeStruct((n_mp * rows, local_cols), BF)],
    )
    query_blocks, own_probs = blocks[:n_mp], blocks[n_mp:]
    first_probs = to_owners(own_probs)
    out_blocks, first_probs, query_blocks = lax.optimization_barrier(
        (out_blocks, first_probs, query_blocks)
    )
    query_blocks = to_owners(query_blocks)
    out_fold, *outs = on_chip(
        functools.partial(first_kernel, n_mp, chunks, share),
        [whole_fold] + [wide] * (2 * chunks),
        factor,
        decoder_in,
        *first_probs,
        *out_blocks,
    )
    helds, followings = outs[:chunks], outs[chunks:]
    (query_fold,) = on_chip(
        functools.partial(pack_kernel, n_mp), [whole_fold], *query_blocks
    )
    folds = (query_fold, out_fold)
    for step in range(1, sections):
        cames = [lax.ppermute(part, "section", [(step - 1, step)]) for part in followings]
        if step < sections - 1:
            for c in range(chunks):
                helds[c], followings[c] = on_chip(
                    functools.partial(forward_kernel, step, c, src),
                    [wide, wide],
                                cames[c],
                    helds[c],
                    masks[c],
                    factor,
                    *folds,
                )
    currents, probs, grads, befores = [], [], [], []
    for c in range(chunks):
        results = on_chip(
            functools.partial(turn_kernel, sections - 1, c, src, share),
            [wide, (masks[c].shape, F32), wide, wide],
                cames[c],
            helds[c],
            masks[c],
            factor,
            *folds,
            cotangent,
        )
        for kept, result in zip((currents, probs, grads, befores), results, strict=True):
            kept.append(result)

    out_cols = dim // n_mp
    for step in range(sections - 1, 0, -1):
        cames = [lax.ppermute(part, "section", [(step, step - 1)]) for part in befores]
        if step == 3:
            whole, *parts = on_chip(
                functools.partial(outputs_kernel, n_mp, chunks),
                [((rows, dim), BF)] + [((rows, out_cols), BF)] * n_mp,
                        factor,
                out_fold,
                *currents,
                *probs,
            )
            cames, whole, parts = lax.optimization_barrier((cames, whole, parts))
        if step == 2:
            cames, parts, evens = lax.optimization_barrier(
                (cames, to_owners(parts), even_mp(whole))
            )
        if step == 1:
            (section_out,) = on_chip(
                functools.partial(order_kernel, n_mp),
                [((n_mp, rows, out_cols), BF)],
                        *parts,
            )
            query, own_probs = on_chip(
                functools.partial(query_kernel, n_mp, src, heads),
                [((n_mp * rows, local_cols), BF), (own_allowed.shape, F32)],
                        keys,
                wq,
                own_allowed,
                *with_odd_mp(evens),
            )
            cames, section_out, query, own_probs = lax.optimization_barrier(
                (cames, section_out, query, own_probs)
            )
            break
        for c in range(chunks):
            grads[c], befores[c] = on_chip(
                functools.partial(backward_kernel, step - 1, c, src),
                [wide, wide],
                        cames[c],
                grads[c],
                probs[c],
                factor,
                *folds,
            )
    gathered = []
    for c in range(chunks):
        if gathered:
            cames[c], gathered[-1][1] = lax.optimization_barrier((cames[c], gathered[-1][1]))
        (d_out,) = on_chip(
            functools.partial(dropped_kernel, 0, c), [wide], cames[c], grads[c], factor
        )
        gathered.append(over_mp(d_out))
    every_d_out = [gathered[c][j] for j in range(n_mp) for c in range(chunks)]
    half_rows = n_mp // 2 * sections * micro_count
    kept, sent = on_chip(
        functools.partial(terms_kernel, n_mp, src, heads),
        [((half_rows, dim), F32), ((half_rows, dim), BF)],
        keys,
        values,
        query,
        own_probs,
        by_micro,
        wk,
        wv,
        wo,
        *every_d_out,
        scratch=[
            jax.ShapeDtypeStruct((n_mp * rows, local_cols), BF),
            jax.ShapeDtypeStruct(*stacked),
            jax.ShapeDtypeStruct(*stacked),
        ],
    )
    half = (kept + swap(sent, "mp", 1).astype(F32)).reshape(n_mp // 2, -1, dim)
    total = half[0]
    for j in range(1, n_mp // 2):
        total = total + swap(half[j].astype(BF), "mp", 2 * j).astype(F32)
    total = total.reshape(sections, micro_count, dim)
    mem_grad = total[0]
    for a in range(1, sections):
        mem_grad = mem_grad + swap(total[a].astype(BF), "section", a).astype(F32)
    return (section_out.reshape(1, micro_count, tgt_rows, out_cols), mem_grad[None])


def solution(mesh):
    return jax.shard_map(
        per_device,
        mesh=mesh,
        in_specs=(
            P(("section", "mp"), "groups", None),
            P("groups", None, None),
            P("groups", None, None),
            P("groups", None),
            P("groups", None),
            P("groups", "section"),
            P("section", None, "mp"),
            P("section", None, "mp"),
            P("section", None, "mp"),
            P("section", "mp", None),
        ),
        out_specs=(P("section", "groups", None, "mp"), P(("section", "mp"), "groups", None)),
        check_vma=False,
    )
```

```python
import functools
import math

import jax
import jax.numpy as jnp
from jax import lax
from jax.experimental import pallas as pl
from jax.experimental.pallas import tpu as pltpu
from jax.sharding import PartitionSpec as P

HD = 256
NEG_FILL = -1e30
KEEP_SCALE = 8.0 / 7.0
BF = jnp.bfloat16
F32 = jnp.float32
MEBI = 1024 * 1024
LIGHT = pl.CostEstimate(flops=1, bytes_accessed=1, transcendentals=0)
NN = (((1,), (0,)), ((), ()))
NT = (((1,), (1,)), ((), ()))
SCALE = 1.0 / math.sqrt(HD)


def shifted_right(source_bits, amount):
    return lax.shift_right_logical(source_bits, jnp.full(source_bits.shape, amount, jnp.int32))


def keep_factor(seed_value, first_row, first_col, shape, col_count):
    rows = first_row + lax.broadcasted_iota(jnp.int32, shape, 0)
    position = rows * col_count + first_col + lax.broadcasted_iota(jnp.int32, shape, 1)
    hashed = position ^ seed_value * 1640531527
    hashed = hashed ^ shifted_right(hashed, 16)
    hashed = hashed * 2146121005
    hashed = hashed ^ shifted_right(hashed, 15)
    hashed = hashed * 1911520717
    hashed = hashed ^ shifted_right(hashed, 16)
    is_kept = shifted_right(hashed, 8) & 7 != 0
    return jnp.where(is_kept, KEEP_SCALE, 0.0).astype(F32)


def factor_kernel(share, seeds, factor):
    rows, dim = factor.shape
    owner = lax.axis_index("mp")
    seed = seeds[lax.div(owner, share), 0]
    first = lax.rem(owner, share) * rows
    width = min(dim, 512)
    for first_col in range(0, dim, width):
        cols = slice(first_col, first_col + width)
        factor[:, cols] = keep_factor(seed, first, first_col, (rows, width), dim)


def tokens_of(owner, share, array, first, count):
    rows = array.shape[1] // share
    first = pl.multiple_of(lax.rem(owner, share) * rows + first, count)
    return array[lax.div(owner, share), pl.ds(first, count)]


def swap(array, axis, k):
    size = lax.axis_size(axis)
    return lax.ppermute(array, axis, [(i, i ^ k) for i in range(size)])


def even_mp(array):
    return [array] + [swap(array, "mp", k) for k in range(2, lax.axis_size("mp"), 2)]


def with_odd_mp(evens):
    pieces = []
    for even in evens:
        pieces += [even, swap(even, "mp", 1)]
    return pieces


def over_mp(array):
    return with_odd_mp(even_mp(array))


def product(left, right, dims):
    return lax.dot_general(left, right, dims, preferred_element_type=F32)


def softmax_down(scores, allowed, src):
    shape = scores.shape
    scores = jnp.where(allowed != 0, scores * SCALE, NEG_FILL).reshape(-1, src, shape[1])
    exp_terms = jnp.exp(scores - jnp.max(scores, axis=1, keepdims=True))
    return (exp_terms / jnp.sum(exp_terms, axis=1, keepdims=True)).reshape(shape)


def softmax_back(probs, d_probs, src):
    shape = probs.shape
    probs = probs.reshape(-1, src, shape[1])
    d_probs = d_probs.reshape(probs.shape)
    inner = jnp.sum(probs * d_probs, axis=1, keepdims=True)
    return (probs * (d_probs - inner) * SCALE).reshape(shape)


def spread(weights, fold):
    return product(jnp.transpose(weights).astype(BF), fold[...], NN)


def picked(step, came, held):
    return jnp.where(lax.axis_index("section") == step, came[...], held[...])


def here_kernel(n, *refs):
    pass


def on_hand(*arrays):
    vmem = pl.BlockSpec(memory_space=pltpu.VMEM)
    size = sum(math.prod(a.shape) * a.dtype.itemsize for a in arrays)
    return pl.pallas_call(
        functools.partial(here_kernel, len(arrays)),
        out_shape=[jax.ShapeDtypeStruct(a.shape, a.dtype) for a in arrays],
        in_specs=[vmem] * len(arrays),
        out_specs=[vmem] * len(arrays),
        input_output_aliases={k: k for k in range(len(arrays))},
        compiler_params=pltpu.CompilerParams(vmem_limit_bytes=size + 2 * MEBI),
    )(*arrays)


def store_folds(part, h, src, cols, folds):
    for k, fold in enumerate(folds):
        fold[h * src : (h + 1) * src, cols] = part[k * src : (k + 1) * src]


def columns(dim):
    width = min(dim, 1024)
    return [slice(first, first + width) for first in range(0, dim, width)]


def values_kernel(n, src, heads, by_owner, wv, wo, *refs):
    pieces, (values, *folds) = refs[:n], refs[n:]
    rows = jnp.concatenate([piece[...] for piece in pieces], axis=0)
    flat = product(rows, wv[...], NN).astype(BF)
    values[...] = product(by_owner[...], flat, NN).astype(BF)
    for h in range(heads):
        head = slice(h * HD, (h + 1) * HD)
        for cols in columns(wo.shape[1]):
            part = product(values[:, head], wo[head, cols], NN).astype(BF)
            store_folds(part, h, src, cols, folds)


def keys_kernel(n, src, heads, share, by_owner, allowed, inputs, wk, wq, *refs):
    pieces, (keys, *outs) = refs[:n], refs[n : 3 * n + 1]
    folds, probs = outs[:n], outs[n:]
    query = refs[3 * n + 1]
    rows = jnp.concatenate([piece[...] for piece in pieces], axis=0)
    flat = product(rows, wk[...], NN).astype(BF)
    keys[...] = product(by_owner[...], flat, NN).astype(BF)
    me = lax.axis_index("mp")
    count = allowed.shape[1]
    tokens = []
    for j in range(n):
        tokens.append(tokens_of(me ^ j, share, inputs, 0, count))
    query[...] = product(jnp.concatenate(tokens, axis=0), wq[...], NN).astype(BF)
    for tile, toks, srcs, cols in heads_of(n, heads, count, src):
        k, h = divmod(tile.start // src, heads)
        own = softmax_down(product(keys[srcs, cols], query[toks, cols], NT), allowed[tile], src)
        probs[k][h * src : (h + 1) * src] = own.astype(BF)
    for h in range(heads):
        head = slice(h * HD, (h + 1) * HD)
        for cols in columns(wq.shape[0]):
            part = product(keys[:, head], wq[cols, head], NT).astype(BF)
            store_folds(part, h, src, cols, folds)


def part_of(array, c, size):
    return array[c * size : (c + 1) * size]


def forward(tokens, allowed, factor, query_fold, out_fold, src):
    probs = softmax_down(product(query_fold[...], tokens, NT), allowed[...], src)
    return (tokens.astype(F32) + factor * spread(probs, out_fold)).astype(BF)


def pack(blocks, fold):
    size = blocks[0].shape[0]
    for k, block in enumerate(blocks):
        fold[k * size : (k + 1) * size] = block[...]


def first_kernel(n, chunks, share, factor, inputs, *refs):
    probs, blocks, (out_fold, *outs) = refs[:n], refs[n : 2 * n], refs[2 * n :]
    helds, following = outs[:chunks], outs[chunks:]
    pack(blocks, out_fold)
    weights = jnp.concatenate([block[...] for block in probs], axis=0).astype(F32)
    kept = factor[...] * spread(weights, out_fold)
    size = kept.shape[0] // chunks
    for c in range(chunks):
        held = tokens_of(lax.axis_index("mp"), share, inputs, c * size, size)
        helds[c][...] = held
        following[c][...] = (held.astype(F32) + kept[c * size : (c + 1) * size]).astype(BF)


def pack_kernel(n, *refs):
    pack(refs[:n], refs[n])


def forward_kernel(
    step, c, src, came, held, allowed, factor, query_fold, out_fold, current, following
):
    tokens = picked(step, came, held)
    current[...] = tokens
    factor = part_of(factor, c, tokens.shape[0])
    following[...] = forward(tokens, allowed, factor, query_fold, out_fold, src)


def backward(probs, grad, factor, query_fold, out_fold, src):
    d_out = (grad.astype(F32) * factor).astype(BF)
    d_scores = softmax_back(probs, product(out_fold[...], d_out, NT), src)
    return (grad.astype(F32) + spread(d_scores, query_fold)).astype(BF)


def turn_kernel(
    step, c, src, share, came, held, allowed, factor, query_fold, out_fold, cotangent, current, kept, grad, before
):
    tokens = picked(step, came, held)
    current[...] = tokens
    probs = softmax_down(product(query_fold[...], tokens, NT), allowed[...], src)
    kept[...] = probs
    factor = part_of(factor, c, tokens.shape[0])
    grad[...] = tokens_of(lax.axis_index("mp"), share, cotangent, c * tokens.shape[0], tokens.shape[0])
    before[...] = backward(probs, grad[...], factor, query_fold, out_fold, src)


def backward_kernel(
    step, c, src, came, held, probs, factor, query_fold, out_fold, current, before
):
    grad = picked(step, came, held)
    current[...] = grad
    factor = part_of(factor, c, grad.shape[0])
    before[...] = backward(probs[...], grad, factor, query_fold, out_fold, src)


def dropped_kernel(step, c, came, held, factor, d_out):
    grad = picked(step, came, held)
    d_out[...] = (grad.astype(F32) * part_of(factor, c, grad.shape[0])).astype(BF)


def outputs_kernel(n, chunks, factor, out_fold, *refs):
    currents, probs, (whole, *parts) = refs[:chunks], refs[chunks : 2 * chunks], refs[2 * chunks :]
    width = parts[0].shape[1]
    size = currents[0].shape[0]
    turned = [jnp.transpose(block[...]).astype(BF) for block in probs]
    turned = jnp.concatenate(turned, axis=0)
    for c in range(chunks):
        whole[c * size : (c + 1) * size] = currents[c][...]
    for j in range(n):
        cols = pl.ds(pl.multiple_of((lax.axis_index("mp") ^ j) * width, width), width)
        summed = product(turned, out_fold[:, cols], NN)
        total = whole[:, cols].astype(F32) + factor[:, cols] * summed
        parts[j][...] = total.astype(BF)


def order_kernel(n, *refs):
    for j in range(n):
        refs[n][lax.axis_index("mp") ^ j] = refs[j][...]


def heads_of(n, heads, rows, src):
    for k in range(n):
        for h in range(heads):
            tile = slice((k * heads + h) * src, (k * heads + h + 1) * src)
            cols = slice(h * HD, (h + 1) * HD)
            yield tile, slice(k * rows, (k + 1) * rows), slice(k * src, (k + 1) * src), cols


def query_kernel(n, src, heads, keys, wq, allowed, *refs):
    pieces, (query, probs) = refs[:n], refs[n:]
    rows = pieces[0].shape[0]
    tokens = jnp.concatenate([piece[...] for piece in pieces], axis=0)
    query[...] = product(tokens, wq[...], NN).astype(BF)
    for tile, toks, srcs, cols in heads_of(n, heads, rows, src):
        scores = product(keys[srcs, cols], query[toks, cols], NT)
        probs[tile] = softmax_down(scores, allowed[tile], src)


def terms_kernel(n, src, heads, keys, values, query, probs, by_micro, wk, wv, wo, *refs):
    pieces, (kept, sent, d_att, d_keys, d_values) = refs[:-5], refs[-5:]
    rows = query.shape[0] // n
    grads = jnp.concatenate([piece[...] for piece in pieces], axis=0)
    d_att[...] = product(grads, wo[...], NT).astype(BF)
    for tile, toks, srcs, cols in heads_of(n, heads, rows, src):
        own = probs[tile]
        d_scores = softmax_back(own, product(values[srcs, cols], d_att[toks, cols], NT), src)
        d_keys[srcs, cols] = product(d_scores.astype(BF), query[toks, cols], NN).astype(BF)
        d_values[srcs, cols] = product(own.astype(BF), d_att[toks, cols], NN).astype(BF)
    key_rows = product(by_micro[...], d_keys[...], NN).astype(BF)
    value_rows = product(by_micro[...], d_values[...], NN).astype(BF)
    size = key_rows.shape[0] // n
    dim = kept.shape[1]
    width = min(dim, 1024)
    for first in range(0, dim, width):
        cols = slice(first, first + width)
        part = product(key_rows, wk[cols], NT) + product(value_rows, wv[cols], NT)
        for k in range(0, n, 2):
            to = slice(k // 2 * size, (k // 2 + 1) * size)
            kept[to, cols] = part[k * size : (k + 1) * size]
            sent[to, cols] = part[(k + 1) * size : (k + 2) * size].astype(BF)


def on_chip(body, outs, *args, scratch=()):
    vmem = pl.BlockSpec(memory_space=pltpu.VMEM)
    outs = [jax.ShapeDtypeStruct(*out) for out in outs]
    size = sum(math.prod(a.shape) * a.dtype.itemsize for a in (*args, *outs, *scratch))
    return pl.pallas_call(
        body,
        out_shape=outs,
        in_specs=[vmem] * len(args),
        out_specs=[vmem] * len(outs),
        scratch_shapes=[pltpu.VMEM(s.shape, s.dtype) for s in scratch],
        compiler_params=pltpu.CompilerParams(vmem_limit_bytes=size + 3 * MEBI),
        cost_estimate=pl.CostEstimate(flops=64 * size, bytes_accessed=size, transcendentals=0),
    )(*args)


def per_device(
    memory, decoder_in, cotangent, src_lengths, tgt_segments, seeds, w_query, w_key, w_value, w_out
):
    micro_count, tgt_rows, dim = decoder_in.shape
    local_cols = w_query.shape[2]
    heads = local_cols // HD
    sections = lax.axis_size("section")
    n_mp = lax.axis_size("mp")
    section = lax.axis_index("section")
    me = lax.axis_index("mp")
    share = n_mp // micro_count
    rows = tgt_rows // share
    src = sections * n_mp
    fold_rows = heads * src
    wq, wk, wv, wo = w_query[0], w_key[0], w_value[0], w_out[0]

    chunks = 2 if rows % 32 == 0 else 1
    wide = ((rows // chunks, dim), BF)

    own = memory.reshape(micro_count, dim)
    over_z = [own if a == 0 else swap(own, "section", a) for a in range(sections)]
    over_z = jnp.concatenate(over_z, axis=0)
    factor = pl.pallas_call(
        functools.partial(factor_kernel, share),
        out_shape=jax.ShapeDtypeStruct((rows, dim), F32),
        in_specs=[pl.BlockSpec(memory_space=pltpu.SMEM)],
        out_specs=pl.BlockSpec(memory_space=pltpu.VMEM),
        compiler_params=pltpu.CompilerParams(vmem_limit_bytes=4 * MEBI),
        cost_estimate=LIGHT,
    )(seeds)
    over_z, factor, wv_near, wo_near = lax.optimization_barrier(
        (over_z, factor, *on_hand(wv, wo))
    )
    pieces = over_mp(over_z)

    to_row = jnp.arange(n_mp * src, dtype=jnp.int32)[:, None]
    from_row = jnp.arange(src * micro_count, dtype=jnp.int32)[None, :]
    by_owner = (to_row % src == from_row // micro_count) & (
        (me ^ (to_row // src)) // share == from_row % micro_count
    )
    by_owner = by_owner.astype(BF)

    stacked = ((n_mp * src, local_cols), BF)
    block = ((fold_rows, dim), BF)
    whole_fold = ((n_mp * fold_rows, dim), BF)
    def row_ids(device):
        j = jnp.arange(n_mp, dtype=jnp.int32)[:, None]
        a = jnp.arange(sections, dtype=jnp.int32)[None, :]
        return ((section ^ a) * n_mp + (device ^ j)).reshape(src)

    doc_ends = jnp.cumsum(src_lengths, axis=1)

    def allowed_of(owner, heads_owner):
        micro = owner // share
        ends = lax.dynamic_index_in_dim(doc_ends, micro, 0, keepdims=False)
        segments = lax.dynamic_index_in_dim(tgt_segments, micro, 0, keepdims=False)
        segments = lax.dynamic_slice_in_dim(segments, (owner % share) * rows, rows, 0)
        docs = jnp.sum((ends[None, :] <= row_ids(heads_owner)[:, None]).astype(jnp.int32), axis=1)
        return docs[:, None] == segments[None, :]

    def every_head(blocks):
        blocks = jnp.broadcast_to(jnp.stack(blocks)[:, None], (n_mp, heads, src, rows))
        return blocks.astype(jnp.int32).reshape(n_mp * fold_rows, rows)

    own_allowed = every_head([allowed_of(me ^ j, me) for j in range(n_mp)])
    allowed = every_head([allowed_of(me, me ^ k) for k in range(n_mp)])
    size = rows // chunks
    masks = [lax.slice_in_dim(allowed, c * size, (c + 1) * size, axis=1) for c in range(chunks)]
    own_allowed, by_owner, by_micro, masks = lax.optimization_barrier(
        (own_allowed, by_owner, by_owner.T, masks)
    )
    values, *out_blocks = on_chip(
        functools.partial(values_kernel, n_mp, src, heads),
        [stacked] + [block] * n_mp,
        by_owner,
        wv_near,
        wo_near,
        *pieces,
    )
    def to_owners(blocks):
        return [part if j == 0 else swap(part, "mp", j) for j, part in enumerate(blocks)]

    out_blocks = to_owners(out_blocks)
    out_blocks[1], pieces = lax.optimization_barrier((out_blocks[1], pieces))
    keys, *blocks = on_chip(
        functools.partial(keys_kernel, n_mp, src, heads, share),
        [stacked] + [block] * n_mp + [((fold_rows, rows), BF)] * n_mp,
        by_owner,
        own_allowed,
        decoder_in,
        wk,
        wq,
        *pieces,
        scratch=[jax.ShapeDtypeStruct((n_mp * rows, local_cols), BF)],
    )
    query_blocks, own_probs = blocks[:n_mp], blocks[n_mp:]
    first_probs = to_owners(own_probs)
    out_blocks, first_probs, query_blocks = lax.optimization_barrier(
        (out_blocks, first_probs, query_blocks)
    )
    query_blocks = to_owners(query_blocks)
    out_fold, *outs = on_chip(
        functools.partial(first_kernel, n_mp, chunks, share),
        [whole_fold] + [wide] * (2 * chunks),
        factor,
        decoder_in,
        *first_probs,
        *out_blocks,
    )
    helds, followings = outs[:chunks], outs[chunks:]
    (query_fold,) = on_chip(
        functools.partial(pack_kernel, n_mp), [whole_fold], *query_blocks
    )
    folds = (query_fold, out_fold)
    for step in range(1, sections):
        cames = [lax.ppermute(part, "section", [(step - 1, step)]) for part in followings]
        if step < sections - 1:
            for c in range(chunks):
                helds[c], followings[c] = on_chip(
                    functools.partial(forward_kernel, step, c, src),
                    [wide, wide],
                                cames[c],
                    helds[c],
                    masks[c],
                    factor,
                    *folds,
                )
    currents, probs, grads, befores = [], [], [], []
    for c in range(chunks):
        results = on_chip(
            functools.partial(turn_kernel, sections - 1, c, src, share),
            [wide, (masks[c].shape, F32), wide, wide],
                cames[c],
            helds[c],
            masks[c],
            factor,
            *folds,
            cotangent,
        )
        for kept, result in zip((currents, probs, grads, befores), results, strict=True):
            kept.append(result)

    out_cols = dim // n_mp
    for step in range(sections - 1, 0, -1):
        cames = [lax.ppermute(part, "section", [(step, step - 1)]) for part in befores]
        if step == 3:
            whole, *parts = on_chip(
                functools.partial(outputs_kernel, n_mp, chunks),
                [((rows, dim), BF)] + [((rows, out_cols), BF)] * n_mp,
                        factor,
                out_fold,
                *currents,
                *probs,
            )
            cames, whole, parts = lax.optimization_barrier((cames, whole, parts))
        if step == 2:
            cames, parts, evens = lax.optimization_barrier(
                (cames, to_owners(parts), even_mp(whole))
            )
        if step == 1:
            (section_out,) = on_chip(
                functools.partial(order_kernel, n_mp),
                [((n_mp, rows, out_cols), BF)],
                        *parts,
            )
            query, own_probs = on_chip(
                functools.partial(query_kernel, n_mp, src, heads),
                [((n_mp * rows, local_cols), BF), (own_allowed.shape, F32)],
                        keys,
                wq,
                own_allowed,
                *with_odd_mp(evens),
            )
            cames, section_out, query, own_probs = lax.optimization_barrier(
                (cames, section_out, query, own_probs)
            )
            break
        for c in range(chunks):
            grads[c], befores[c] = on_chip(
                functools.partial(backward_kernel, step - 1, c, src),
                [wide, wide],
                        cames[c],
                grads[c],
                probs[c],
                factor,
                *folds,
            )
    gathered = []
    for c in range(chunks):
        (d_out,) = on_chip(
            functools.partial(dropped_kernel, 0, c), [wide], cames[c], grads[c], factor
        )
        gathered.append(over_mp(d_out))
    every_d_out = [gathered[c][j] for j in range(n_mp) for c in range(chunks)]
    half_rows = n_mp // 2 * sections * micro_count
    kept, sent = on_chip(
        functools.partial(terms_kernel, n_mp, src, heads),
        [((half_rows, dim), F32), ((half_rows, dim), BF)],
        keys,
        values,
        query,
        own_probs,
        by_micro,
        wk,
        wv,
        wo,
        *every_d_out,
        scratch=[
            jax.ShapeDtypeStruct((n_mp * rows, local_cols), BF),
            jax.ShapeDtypeStruct(*stacked),
            jax.ShapeDtypeStruct(*stacked),
        ],
    )
    half = (kept + swap(sent, "mp", 1).astype(F32)).reshape(n_mp // 2, -1, dim)
    total = half[0]
    for j in range(1, n_mp // 2):
        total = total + swap(half[j].astype(BF), "mp", 2 * j).astype(F32)
    total = total.reshape(sections, micro_count, dim)
    mem_grad = total[0]
    for a in range(1, sections):
        mem_grad = mem_grad + swap(total[a].astype(BF), "section", a).astype(F32)
    return (section_out.reshape(1, micro_count, tgt_rows, out_cols), mem_grad[None])


def solution(mesh):
    return jax.shard_map(
        per_device,
        mesh=mesh,
        in_specs=(
            P(("section", "mp"), "groups", None),
            P("groups", None, None),
            P("groups", None, None),
            P("groups", None),
            P("groups", None),
            P("groups", "section"),
            P("section", None, "mp"),
            P("section", None, "mp"),
            P("section", None, "mp"),
            P("section", "mp", None),
        ),
        out_specs=(P("section", "groups", None, "mp"), P(("section", "mp"), "groups", None)),
        check_vma=False,
    )
```
